512 devices in a mesh: ctx: 64 (over y, z_hi, core), head: 8 (over x, z_lo).
Axes of the slice: x: 4, y: 8, z: 8 (z_hi: 4, z_lo: 2; z = z_hi * 2 + z_lo), core: 2. Of those that a mesh axis runs over, the one named last changes fastest.
Arguments:
- queries: bfloat16 [1, 65536, 1024], P(None, ('ctx', 'head')), may hold values from -150 to 150
- keys: bfloat16 [1, 65536, 1024], P(None, ('ctx', 'head')), may hold values from -32 to 32
- values: bfloat16 [1, 65536, 1024], P(None, ('ctx', 'head')), may hold values from -6 to 6
- rates: float32 [1, 8, 65536], P(None, 'head', 'ctx'), may hold values from 0.0002 to 0.004
- tail_keys: bfloat16 [32768, 1024], P('ctx', 'head'), may hold values from -6 to 6
- tail_values: bfloat16 [32768, 1024], P('ctx', 'head'), may hold values from -6 to 6
- state_in_gu: float32 [64, 8, 2, 128, 256], P('ctx', 'head'), may hold values from -0.5 to 0.5
- state_in_down: float32 [64, 8, 256, 128], P('ctx', 'head'), may hold values from -0.375 to 0.375
- fresh_gu: float32 [8, 2, 128, 256], P('head'), may hold values from -0.5 to 0.5
- fresh_down: float32 [8, 256, 128], P('head'), may hold values from -0.375 to 0.375
- out_gain: float32 [1024], P('head'), may hold values from 0.1 to 1.9
- seq_ids: int32 [64, 2], replicated, may hold values from 0 to 127, as said below
- live_lengths: int32 [64, 1], replicated, may hold values from 1 to 1024, as said below
Outputs:
- mixed: bfloat16 [1, 65536, 1024], P(None, ('ctx', 'head'))
- state_out_gu: float32 [64, 8, 2, 128, 256], P('ctx', 'head')
- state_out_down: float32 [64, 8, 256, 128], P('ctx', 'head')
The draws below stay inside these ranges and needn't reach their ends.
Inputs may be any that keep to these rules, and one draw needn't show every extreme that they name: `seq_ids`: block (c, t + 1) continues the sequence of block ((c - 1) mod 64, t) exactly when their numbers agree, else it begins a new sequence; different sequences have different numbers. `live_lengths`: only a block whose successor (device c + 1 mod 64, step t + 1) begins a new sequence is shorter than 1024; its live tokens are the first ones.
All inputs are finite; a program needn't handle non-finite values.
Results may differ from the reference program's by a relative error of at most 0.0028.
Values may be sent and summed in bfloat16 or wider, within the bound.
A program may use at most 64 MiB of HBM per device.

```python
import math
import jax
import jax.numpy as jnp
from jax import lax

HD = 128
HID = 256
BLOCK = 1024
WIN = 512
STEPS = 1
HEADS = 8
FEATURES = 1024
TOK_STEP = 65536
N_CTX = 64


def paired_draw(key):
    inner = jax.random.fold_in(key, 11)
    streams = jax.random.split(inner, 6)
    shape = (STEPS, TOK_STEP, HEADS, HD)
    base_query = jnp.clip(jax.random.normal(streams[0], shape, jnp.float32), -4.0, 4.0)
    base_key = jnp.clip(jax.random.normal(streams[1], shape, jnp.float32), -4.0, 4.0)
    row_query = jnp.exp(jax.random.uniform(streams[2], (STEPS, TOK_STEP, HEADS, 1), jnp.float32, math.log(0.32), math.log(3.2)))
    col_query = jnp.exp(jax.random.uniform(streams[3], (HEADS, HD), jnp.float32, math.log(0.6), math.log(1.8)))
    row_key = jnp.exp(jax.random.uniform(streams[4], (STEPS, TOK_STEP, HEADS, 1), jnp.float32, math.log(0.32), math.log(3.2)))
    col_key = jnp.exp(jax.random.uniform(streams[5], (HEADS, HD), jnp.float32, math.log(0.6), math.log(1.8)))
    query_draw = base_query * row_query * col_query
    key_draw = base_key * row_key * col_key
    query_draw = query_draw.reshape(STEPS, TOK_STEP, HEADS * HD).astype(jnp.bfloat16)
    key_draw = key_draw.reshape(STEPS, TOK_STEP, HEADS * HD).astype(jnp.bfloat16)
    return (query_draw, key_draw)


def draw_queries(key, part):
    return paired_draw(key)[0]


def draw_keys(key, part):
    return paired_draw(key)[1]


def chain_layout(key):
    inner = jax.random.fold_in(key, 23)
    streams = jax.random.split(inner, 2)
    ctx_count = TOK_STEP // BLOCK
    starts = jax.random.randint(streams[0], (ctx_count, STEPS), 0, 10) < 3
    starts = starts.at[2, 0].set(True).at[1, 0].set(False).at[ctx_count - 1, STEPS - 1].set(True)
    for column in range(STEPS):
        starts = starts.at[(ctx_count - column) % ctx_count, column].set(False)
    column_ids = jnp.arange(1, STEPS + 1, dtype=jnp.int32)
    marks = jnp.where(starts, column_ids[None, :], 0)
    recent = lax.cummax(marks, axis=1)
    recent = jnp.concatenate([jnp.zeros((ctx_count, 1), jnp.int32), recent], axis=1)
    chain_ids = jnp.arange(ctx_count, dtype=jnp.int32)[:, None] * (STEPS + 1) + recent
    is_last = jnp.concatenate([starts[:, 1:], jnp.zeros((ctx_count, 1), bool)], axis=1)
    ragged = jax.random.randint(streams[1], (ctx_count, STEPS), 1, BLOCK + 1)
    chain_lengths = jnp.where(is_last, ragged, BLOCK)
    seq_columns = [jnp.roll(chain_ids[:, column], column - 1) for column in range(STEPS + 1)]
    length_columns = [jnp.roll(chain_lengths[:, column], column) for column in range(STEPS)]
    return (jnp.stack(seq_columns, axis=1).astype(jnp.int32), jnp.stack(length_columns, axis=1).astype(jnp.int32))


def draw_seq_ids(key, part):
    return chain_layout(key)[0]


def draw_live_lengths(key, part):
    return chain_layout(key)[1]


def levels(rng, shape, cuts, least, top_value):
    def one(dim, shards_of):
        draws = jax.random.uniform(jax.random.fold_in(jax.random.fold_in(rng, 6), dim), (shards_of,), jnp.float32, least / len(cuts), top_value / len(cuts))
        return jnp.repeat(jnp.exp(draws), shape[dim] // shards_of).reshape((-1,) + (1,) * (len(shape) - dim - 1))

    loudness = one(*cuts[0])
    for cut in cuts[1:]:
        loudness = loudness * one(*cut)
    return loudness


def gaussian(key, extent, spread, reach, shards=(), kind=jnp.bfloat16):
    values = spread * jax.random.normal(key, extent, jnp.float32)
    if shards:
        values = values * levels(key, extent, shards, -0.22, 0.18)
    return jnp.clip(values, -reach, reach).astype(kind)


def setup_inputs(seed: int = 0) -> dict:
    key_of = jax.random.split(jax.random.key(seed), 14)
    queries = draw_queries(jax.random.fold_in(key_of[13], 71), 0)
    keys = draw_keys(jax.random.fold_in(key_of[13], 71), 0)
    values = gaussian(key_of[2], (STEPS, TOK_STEP, FEATURES), 1.0, 6.0, ((1, 512),))
    rates = jnp.clip(jnp.exp(math.log(0.004) - 2.9957323 * jax.random.uniform(key_of[3], (STEPS, HEADS, TOK_STEP), jnp.float32) ** levels(key_of[3], (STEPS, HEADS, TOK_STEP), ((1, 8), (2, 64)), -0.2, 0.2)), 0.0002, 0.004)
    tail_keys = gaussian(key_of[4], (N_CTX * WIN, FEATURES), 1.0, 6.0, ((0, 64), (1, 8)))
    tail_values = gaussian(key_of[5], (N_CTX * WIN, FEATURES), 1.0, 6.0, ((0, 64), (1, 8)))
    state_in_gu = gaussian(key_of[6], (N_CTX, HEADS, 2, HD, HID), HD ** -0.5, 0.5, ((0, 64), (1, 8)), jnp.float32)
    state_in_down = gaussian(key_of[7], (N_CTX, HEADS, HID, HD), HID ** -0.5, 0.375, ((0, 64), (1, 8)), jnp.float32)
    fresh_gu = gaussian(key_of[8], (HEADS, 2, HD, HID), HD ** -0.5, 0.5, ((0, 8),), jnp.float32)
    fresh_down = gaussian(key_of[9], (HEADS, HID, HD), HID ** -0.5, 0.375, ((0, 8),), jnp.float32)
    out_gain = jnp.clip(1.0 + 0.18 * jax.random.normal(key_of[10], (FEATURES,), jnp.float32), 0.1, 1.9)
    seq_ids = draw_seq_ids(jax.random.fold_in(key_of[13], 71), 0)
    live_lengths = draw_live_lengths(jax.random.fold_in(key_of[13], 71), 0)
    return {"queries": queries, "keys": keys, "values": values, "rates": rates, "tail_keys": tail_keys, "tail_values": tail_values, "state_in_gu": state_in_gu, "state_in_down": state_in_down, "fresh_gu": fresh_gu, "fresh_down": fresh_down, "out_gain": out_gain, "seq_ids": seq_ids, "live_lengths": live_lengths}


epsilon = 1e-06

def highest(left, right):
    return jnp.dot(left, right, precision=lax.Precision.HIGHEST)

def rms_rows(matrix):
    return matrix / jnp.sqrt(lax.optimization_barrier(jnp.mean(matrix * matrix, axis=-1, keepdims=True)) + epsilon)

def renormed(old_weight, new_weight):
    old_scale = jnp.sqrt(lax.optimization_barrier(jnp.mean(old_weight * old_weight, axis=0, keepdims=True)) + epsilon)
    new_scale = jnp.sqrt(lax.optimization_barrier(jnp.mean(new_weight * new_weight, axis=0, keepdims=True)) + epsilon)
    return new_weight * (old_scale / new_scale)

def fast_block(block_q, block_k, block_v, rate_row, prior_keys, prior_values, gate_up, down_proj, fresh_pair, fresh_proj, head_gain, length, linked):
    block_len = block_q.shape[0]
    window = prior_keys.shape[0]
    head_dim = block_q.shape[1]
    gate_up = jnp.where(linked, gate_up, fresh_pair)
    down_proj = jnp.where(linked, down_proj, fresh_proj)
    joined_keys = jnp.concatenate([prior_keys, block_k], axis=0)
    joined_values = jnp.concatenate([prior_values, block_v], axis=0)
    row_index = jnp.arange(window)[:, None]
    col_index = jnp.arange(2 * window)[None, :]
    pieces = []
    for offset in range(0, block_len, window):
        query_pos = offset + row_index
        key_pos = offset - window + col_index
        allowed = (key_pos <= query_pos) & (key_pos > query_pos - window) & ((key_pos < length) | (key_pos == query_pos)) & ((key_pos >= 0) | linked)
        scores = jnp.dot(block_q[offset:offset + window], joined_keys[offset:offset + 2 * window].T, preferred_element_type=jnp.float32) * (1.0 / math.sqrt(head_dim))
        scores = jnp.where(allowed, scores, -1e+30)
        largest = lax.optimization_barrier(jnp.max(scores, axis=-1, keepdims=True))
        exponent = jnp.exp(scores - largest)
        weights = (exponent / lax.optimization_barrier(jnp.sum(exponent, axis=-1, keepdims=True))).astype(jnp.bfloat16)
        pieces.append(jnp.dot(weights, joined_values[offset:offset + 2 * window], preferred_element_type=jnp.float32))
    attended = jnp.concatenate(pieces, axis=0)
    query_unit = rms_rows(block_q.astype(jnp.float32))
    key_unit = rms_rows(block_k.astype(jnp.float32))
    w_gate = gate_up[0]
    w_up = gate_up[1]
    fast_out = highest(jax.nn.silu(highest(query_unit, w_gate)) * highest(query_unit, w_up), down_proj)
    live_rows = (jnp.arange(block_len) < length).astype(jnp.float32)[:, None]
    mixed = ((attended + rms_rows(fast_out) * head_gain) * live_rows).astype(jnp.bfloat16)
    key_gate = highest(key_unit, w_gate)
    key_up = highest(key_unit, w_up)
    gate_sigmoid = jax.nn.sigmoid(key_gate)
    gate_act = key_gate * gate_sigmoid
    out_grad = -(rate_row[:, None] * live_rows) * block_v.astype(jnp.float32)
    grad_down = highest((gate_act * key_up).T, out_grad)
    hidden_grad = highest(out_grad, down_proj.T)
    grad_up = highest(key_unit.T, hidden_grad * gate_act)
    grad_gate = highest(key_unit.T, hidden_grad * key_up * gate_sigmoid * (1.0 + key_gate * (1.0 - gate_sigmoid)))
    new_pair = jnp.stack([renormed(w_gate, w_gate - grad_gate), renormed(w_up, w_up - grad_up)])
    new_down = renormed(down_proj, down_proj - grad_down)
    return (mixed, new_pair, new_down)

def reference(queries, keys, values, rates, tail_keys, tail_values, state_in_gu, state_in_down, fresh_gu, fresh_down, out_gain, seq_ids, live_lengths):

    def by_head(array):
        return array.reshape(STEPS, N_CTX, BLOCK, HEADS, HD).transpose(0, 1, 3, 2, 4)
    query_heads = by_head(queries)
    key_heads = by_head(keys)
    value_heads = by_head(values)
    rate_heads = rates.reshape(STEPS, HEADS, N_CTX, BLOCK).transpose(0, 2, 1, 3)
    tail_key_heads = tail_keys.reshape(N_CTX, WIN, HEADS, HD).transpose(0, 2, 1, 3)
    tail_value_heads = tail_values.reshape(N_CTX, WIN, HEADS, HD).transpose(0, 2, 1, 3)
    head_gains = out_gain.reshape(HEADS, HD)
    apply_heads = jax.vmap(fast_block, in_axes=(0, 0, 0, 0, 0, 0, 0, 0, 0, 0, 0, None, None))

    def per_device(packed):
        return apply_heads(packed[0], packed[1], packed[2], packed[3], packed[4], packed[5], packed[6], packed[7], fresh_gu, fresh_down, head_gains, packed[8], packed[9])
    gate_up = state_in_gu
    down_proj = state_in_down
    results = []
    for wave_step in range(STEPS):
        if wave_step == 0:
            source_keys = tail_key_heads
            source_values = tail_value_heads
        else:
            source_keys = key_heads[wave_step - 1][:, :, BLOCK - WIN:]
            source_values = value_heads[wave_step - 1][:, :, BLOCK - WIN:]
        prior_keys = jnp.roll(source_keys, 1, axis=0)
        prior_values = jnp.roll(source_values, 1, axis=0)
        moved_pair = jnp.roll(gate_up, 1, axis=0)
        moved_proj = jnp.roll(down_proj, 1, axis=0)
        linked = seq_ids[:, wave_step + 1] == jnp.roll(seq_ids[:, wave_step], 1)
        lengths = live_lengths[:, wave_step]
        mixed_step, gate_up, down_proj = lax.map(per_device, (query_heads[wave_step], key_heads[wave_step], value_heads[wave_step], rate_heads[wave_step], prior_keys, prior_values, moved_pair, moved_proj, lengths, linked))
        results.append(mixed_step)
    mixed = jnp.stack(results).transpose(0, 1, 3, 2, 4).reshape(STEPS, N_CTX * BLOCK, HEADS * HD)
    return (mixed, gate_up, down_proj)
```

```python
import math

import jax
import jax.numpy as jnp
from jax import lax
from jax.experimental import pallas as pl
from jax.experimental.pallas import tpu as pltpu
from jax.sharding import PartitionSpec as P

MESH = pl.DeviceIdType.MESH
EPS = 1e-06
NEG = -1e30
HD = 128
HID = 256
BLOCK = 1024
WIN = 512
TILE = 256
X_SIZE = 4
Z_SIZE = 2
PEERS = tuple((dx, dz) for dz in (1, 0) for dx in (2, 1, 3, 0) if (dx, dz) != (0, 0))


def nt(left, right):
    return lax.dot_general(left, right, (((1,), (1,)), ((), ())), preferred_element_type=jnp.float32)


def nn(left, right):
    return jnp.dot(left, right, preferred_element_type=jnp.float32)


def split(matrix):
    high = matrix.astype(jnp.bfloat16)
    low = (matrix - high.astype(jnp.float32)).astype(jnp.bfloat16)
    return high, low


def sigmoid(x):
    return 0.5 * jnp.tanh(0.5 * x) + 0.5


def kernel(
    ctx_count,
    q_ref, k_ref, v_ref, rate_ref, tail_k_ref, tail_v_ref, gu_ref, down_ref,
    fresh_gu_ref, fresh_down_ref, gain_ref, seq_ref, len_ref,
    mixed_ref, gu_out_ref, down_out_ref,
    q_buf, k_buf, v_buf, gu_buf, down_buf, fgu_buf, fdown_buf, out_buf, part_buf,
    local_sem, send_sem, recv_sem, out_send_sem, out_recv_sem,
):
    c = lax.axis_index("ctx")
    h = lax.axis_index("head")
    succ = lax.rem(c + 1, ctx_count)
    pred = lax.rem(c + ctx_count - 1, ctx_count)
    hx, hz = h // Z_SIZE, lax.rem(h, Z_SIZE)
    to_peer = [
        lax.rem(hx + dx, X_SIZE) * Z_SIZE + lax.rem(hz + dz, Z_SIZE) for dx, dz in PEERS
    ]
    from_peer = [
        lax.rem(hx + X_SIZE - dx, X_SIZE) * Z_SIZE + lax.rem(hz + dz, Z_SIZE) for dx, dz in PEERS
    ]
    n_peer = len(PEERS)

    barrier = pltpu.get_barrier_semaphore()
    for peer in to_peer:
        pl.semaphore_signal(barrier, inc=1, device_id=(c, peer), device_id_type=MESH)
    for other in (succ, pred):
        pl.semaphore_signal(barrier, inc=1, device_id=(other, h), device_id_type=MESH)

    def block(index):
        return pl.ds(pl.multiple_of(index * HD, HD), HD)

    def rows(index, base):
        return pl.ds(pl.multiple_of(base + index * HD, HD), HD)

    streams = ((k_ref, k_buf, WIN), (v_ref, v_buf, WIN), (q_ref, q_buf, 0))
    local = []
    for n, (src, dst, base) in enumerate(streams):
        local.append(
            pltpu.make_async_copy(src.at[0, :, block(h)], dst.at[rows(h, base)], local_sem.at[n])
        )
    local.append(pltpu.make_async_copy(fresh_gu_ref.at[0], fgu_buf, local_sem.at[3]))
    local.append(pltpu.make_async_copy(fresh_down_ref.at[0], fdown_buf, local_sem.at[4]))
    for copy in local:
        copy.start()

    pl.semaphore_wait(barrier, n_peer + 2)

    sends = []
    receives = {}

    def remote(name, src, dst, there, sem, here=None):
        copy = pltpu.make_async_remote_copy(
            src_ref=src, dst_ref=dst, send_sem=send_sem.at[sem], recv_sem=recv_sem.at[sem],
            device_id=there, device_id_type=MESH,
        )
        copy.start()
        sends.append(copy)
        arriving = copy if here is None else pltpu.make_async_remote_copy(
            src_ref=src, dst_ref=here, send_sem=send_sem.at[sem], recv_sem=recv_sem.at[sem],
            device_id=there, device_id_type=MESH,
        )
        receives.setdefault(name, []).append(arriving)

    sem = 0
    for n, (src, dst, base) in enumerate(streams):
        for out, back in zip(to_peer, from_peer):
            remote(
                "tokens", src.at[0, :, block(out)], dst.at[rows(h, base)], (c, out), sem,
                dst.at[rows(back, base)],
            )
            sem += 1
    remote("state", gu_ref.at[0, 0], gu_buf, (succ, h), sem)
    remote("state", down_ref.at[0, 0], down_buf, (succ, h), sem + 1)
    remote("tails", tail_k_ref, k_buf.at[pl.ds(0, WIN)], (succ, h), sem + 2)
    remote("tails", tail_v_ref, v_buf.at[pl.ds(0, WIN)], (succ, h), sem + 3)

    length = len_ref[0, c]
    linked = (seq_ref[1, c] == seq_ref[0, pred]).astype(jnp.int32)
    gain = gain_ref[...]
    exponent_scale = math.log2(math.e) / math.sqrt(HD)

    def attend(start):
        cols = WIN + TILE
        scores = nt(q_buf[pl.ds(start, TILE)], k_buf[pl.ds(start, cols)])
        key_pos = start - WIN + lax.broadcasted_iota(jnp.int32, (1, cols), 1)
        usable = jnp.where(key_pos < length, 1, 0) * jnp.where(key_pos >= 0, 1, linked)
        bias = jnp.where(usable > 0, 0.0, NEG)
        row = lax.broadcasted_iota(jnp.int32, (TILE, TILE), 0)
        col = lax.broadcasted_iota(jnp.int32, (TILE, TILE), 1)
        pieces = []
        for at in range(0, cols, TILE):
            own = scores[:, at : at + TILE]
            masked = own + bias[:, at : at + TILE]
            if at == 0:
                masked = jnp.where(col > row, masked, NEG)
            elif at == WIN:
                masked = jnp.where(col < row, masked, jnp.where(col == row, own, NEG))
            pieces.append(masked)
        scores = jnp.concatenate(pieces, axis=1)
        largest = jnp.max(scores, axis=-1, keepdims=True)
        exponent = jnp.exp2((scores - largest) * exponent_scale)
        total = jnp.sum(exponent, axis=-1, keepdims=True)
        weights = (exponent * (1.0 / total)).astype(jnp.bfloat16)
        return nn(weights, v_buf[pl.ds(start, cols)])

    for copy in local:
        copy.wait()
    for copy in receives["tokens"]:
        copy.wait_recv()
    for start in range(WIN, BLOCK, TILE):
        part_buf[pl.ds(start, TILE)] = attend(start)

    for copy in receives["state"]:
        copy.wait_recv()
    w_gate = jnp.where(linked > 0, gu_buf[0], fgu_buf[0])
    w_up = jnp.where(linked > 0, gu_buf[1], fgu_buf[1])
    w_down = jnp.where(linked > 0, down_buf[...], fdown_buf[...])
    down_high, down_low = split(w_down)
    gate_high, gate_low = split(w_gate)
    up_high, up_low = split(w_up)
    in_weights = jnp.concatenate(
        [
            jnp.concatenate([gate_high, up_high], axis=1),
            jnp.concatenate([gate_low, up_low], axis=1),
        ],
        axis=0,
    )
    out_weights = jnp.concatenate([down_high, down_low], axis=1)

    def fast(start):
        own = q_buf[pl.ds(start, TILE)]
        wide = own.astype(jnp.float32)
        unit = lax.rsqrt(jnp.mean(wide * wide, axis=-1, keepdims=True) + EPS)
        hidden = nn(jnp.concatenate([own, own], axis=1), in_weights) * unit
        gate, up = hidden[:, :HID], hidden[:, HID:]
        act_high, act_low = split(gate * sigmoid(gate) * up)
        both = nn(act_high, out_weights)
        result = both[:, :HD] + both[:, HD:] + nn(act_low, down_high)
        scale = lax.rsqrt(jnp.mean(result * result, axis=-1, keepdims=True) + EPS)
        return result * scale * gain

    def finish(start, value):
        live = (start + lax.broadcasted_iota(jnp.int32, (TILE, 1), 0)) < length
        out_buf[pl.ds(start, TILE)] = jnp.where(live, value, 0.0).astype(jnp.bfloat16)

    for start in range(WIN, BLOCK, TILE):
        finish(start, part_buf[pl.ds(start, TILE)] + fast(start))
    for start in range(0, WIN, TILE):
        part_buf[pl.ds(start, TILE)] = fast(start)

    for copy in receives["tails"]:
        copy.wait_recv()
    for start in range(0, WIN, TILE):
        finish(start, part_buf[pl.ds(start, TILE)] + attend(start))

    out_sends, out_receives = [], []
    own_part = pltpu.make_async_copy(
        out_buf.at[rows(h, 0)], mixed_ref.at[0, :, block(h)], local_sem.at[5]
    )
    for n, (out, back) in enumerate(zip(to_peer, from_peer)):
        copy = pltpu.make_async_remote_copy(
            src_ref=out_buf.at[rows(out, 0)], dst_ref=mixed_ref.at[0, :, block(h)],
            send_sem=out_send_sem.at[n], recv_sem=out_recv_sem.at[n],
            device_id=(c, out), device_id_type=MESH,
        )
        copy.start()
        out_sends.append(copy)
        out_receives.append(
            pltpu.make_async_remote_copy(
                src_ref=out_buf.at[rows(out, 0)], dst_ref=mixed_ref.at[0, :, block(back)],
                send_sem=out_send_sem.at[n], recv_sem=out_recv_sem.at[n],
                device_id=(c, out), device_id_type=MESH,
            )
        )
    own_part.start()

    key_weights = jnp.concatenate(
        [
            jnp.concatenate(split(w_gate.T), axis=1),
            jnp.concatenate(split(w_up.T), axis=1),
        ],
        axis=0,
    )
    ones = jnp.ones((8, 2 * HD), jnp.bfloat16)
    grad_in = jnp.zeros((2 * HID, HD), jnp.float32)
    grad_down = jnp.zeros((HID, HD), jnp.float32)
    for start in range(0, BLOCK, TILE):
        key = k_buf[pl.ds(WIN + start, TILE)]
        value = v_buf[pl.ds(WIN + start, TILE)]
        wide = key.astype(jnp.float32)
        squares = nt(ones, jnp.concatenate(split(wide * wide), axis=1))[0:1]
        unit = lax.rsqrt(squares * (1.0 / HD) + EPS)
        token = start + lax.broadcasted_iota(jnp.int32, (1, TILE), 1)
        rate = jnp.where(token < length, rate_ref[0, :, pl.ds(start, TILE)], 0.0)
        hidden = nt(key_weights, jnp.concatenate([key, key], axis=1)) * unit
        gate, up = hidden[:HID], hidden[HID:]
        s = sigmoid(gate)
        act = gate * s
        back = nt(out_weights, jnp.concatenate([value, value], axis=1)) * rate
        grad_down += nn((act * up * rate).astype(jnp.bfloat16), value)
        back = back * unit
        factor = jnp.concatenate([back * up * s * (1.0 + gate * (1.0 - s)), back * act], axis=0)
        grad_in += nn(factor.astype(jnp.bfloat16), key)

    def renormed(old, new):
        old_mean = jnp.mean(old * old, axis=0, keepdims=True) + EPS
        new_mean = jnp.mean(new * new, axis=0, keepdims=True) + EPS
        return new * (jnp.sqrt(old_mean) * lax.rsqrt(new_mean))

    gu_out_ref[0, 0, 0] = renormed(w_gate, w_gate + grad_in[:HID].T)
    gu_out_ref[0, 0, 1] = renormed(w_up, w_up + grad_in[HID:].T)
    down_out_ref[0, 0] = renormed(w_down, w_down + grad_down)

    own_part.wait()
    for copy in sends + out_sends:
        copy.wait_send()
    for copy in out_receives:
        copy.wait_recv()


def solution(mesh):
    ctx_count = mesh.shape["ctx"]
    n_remote = 3 * len(PEERS) + 4

    def on_device(
        queries, keys, values, rates, tail_keys, tail_values, state_in_gu, state_in_down,
        fresh_gu, fresh_down, out_gain, seq_ids, live_lengths,
    ):
        hbm = pl.BlockSpec(memory_space=pltpu.HBM)
        vmem = pl.BlockSpec(memory_space=pltpu.VMEM)
        smem = pl.BlockSpec(memory_space=pltpu.SMEM)

        def body(*refs):
            kernel(ctx_count, *refs)

        return pl.pallas_call(
            body,
            name="layer",
            out_shape=(
                jax.ShapeDtypeStruct(queries.shape, jnp.bfloat16),
                jax.ShapeDtypeStruct(state_in_gu.shape, jnp.float32),
                jax.ShapeDtypeStruct(state_in_down.shape, jnp.float32),
            ),
            in_specs=[hbm, hbm, hbm, vmem, hbm, hbm, hbm, hbm, hbm, hbm, vmem, smem, smem],
            out_specs=(vmem, vmem, vmem),
            scratch_shapes=[
                pltpu.VMEM((BLOCK, HD), jnp.bfloat16),
                pltpu.VMEM((WIN + BLOCK, HD), jnp.bfloat16),
                pltpu.VMEM((WIN + BLOCK, HD), jnp.bfloat16),
                pltpu.VMEM((2, HD, HID), jnp.float32),
                pltpu.VMEM((HID, HD), jnp.float32),
                pltpu.VMEM((2, HD, HID), jnp.float32),
                pltpu.VMEM((HID, HD), jnp.float32),
                pltpu.VMEM((BLOCK, HD), jnp.bfloat16),
                pltpu.VMEM((BLOCK, HD), jnp.float32),
                pltpu.SemaphoreType.DMA((6,)),
                pltpu.SemaphoreType.DMA((n_remote,)),
                pltpu.SemaphoreType.DMA((n_remote,)),
                pltpu.SemaphoreType.DMA((len(PEERS),)),
                pltpu.SemaphoreType.DMA((len(PEERS),)),
            ],
            compiler_params=pltpu.CompilerParams(
                collective_id=0, has_side_effects=True
            ),
        )(
            queries, keys, values, rates, tail_keys, tail_values, state_in_gu, state_in_down,
            fresh_gu, fresh_down, out_gain[None], seq_ids.T, live_lengths.T,
        )

    placed = (
        P(None, ("ctx", "head"), None),
        P(None, ("ctx", "head"), None),
        P(None, ("ctx", "head"), None),
        P(None, "head", "ctx"),
        P("ctx", "head"),
        P("ctx", "head"),
        P("ctx", "head", None, None, None),
        P("ctx", "head", None, None),
        P("head", None, None, None),
        P("head", None, None),
        P("head"),
        P(),
        P(),
    )
    return jax.shard_map(
        on_device,
        mesh=mesh,
        in_specs=placed,
        out_specs=(
            P(None, ("ctx", "head"), None),
            P("ctx", "head", None, None, None),
            P("ctx", "head", None, None),
        ),
        check_vma=False,
    )
```

```python
import math

import jax
import jax.numpy as jnp
from jax import lax
from jax.experimental import pallas as pl
from jax.experimental.pallas import tpu as pltpu
from jax.sharding import PartitionSpec as P

MESH = pl.DeviceIdType.MESH
EPS = 1e-06
NEG = -1e30
HD = 128
HID = 256
BLOCK = 1024
WIN = 512
TILE = 256
X_SIZE = 4
Z_SIZE = 2
STEPS = 32767.0
PEERS = tuple((dx, dz) for dz in (1, 0) for dx in (2, 1, 3, 0) if (dx, dz) != (0, 0))


def nt(left, right):
    return lax.dot_general(left, right, (((1,), (1,)), ((), ())), preferred_element_type=jnp.float32)


def nn(left, right):
    return jnp.dot(left, right, preferred_element_type=jnp.float32)


def split(matrix):
    high = matrix.astype(jnp.bfloat16)
    low = (matrix - high.astype(jnp.float32)).astype(jnp.bfloat16)
    return high, low


def sigmoid(x):
    return 0.5 * jnp.tanh(0.5 * x) + 0.5


def kernel(
    ctx_count,
    q_ref, k_ref, v_ref, rates_ref, tail_k_ref, tail_v_ref, gu_ref, down_ref,
    fresh_gu_ref, fresh_down_ref, gains_ref, seqs_ref, lens_ref,
    mixed_ref, gu_out_ref, down_out_ref,
    q_buf, k_buf, v_buf, gu_buf, down_buf, fgu_buf, fdown_buf, out_buf, part_buf,
    gu_code, down_code, scale_code, gu_in, down_in, scale_in,
    rate_ref, gain_ref, seq_ref, len_ref,
    local_sem, send_sem, recv_sem, out_send_sem, out_recv_sem,
):
    c = lax.axis_index("ctx")
    h = lax.axis_index("head")
    succ = lax.rem(c + 1, ctx_count)
    pred = lax.rem(c + ctx_count - 1, ctx_count)
    hx, hz = h // Z_SIZE, lax.rem(h, Z_SIZE)
    to_peer = [
        lax.rem(hx + dx, X_SIZE) * Z_SIZE + lax.rem(hz + dz, Z_SIZE) for dx, dz in PEERS
    ]
    from_peer = [
        lax.rem(hx + X_SIZE - dx, X_SIZE) * Z_SIZE + lax.rem(hz + dz, Z_SIZE) for dx, dz in PEERS
    ]
    n_peer = len(PEERS)

    barrier = pltpu.get_barrier_semaphore()
    for peer in to_peer:
        pl.semaphore_signal(barrier, inc=1, device_id=(c, peer), device_id_type=MESH)
    pl.semaphore_signal(barrier, inc=1, device_id=(pred, h), device_id_type=MESH)

    def block(index):
        return pl.ds(pl.multiple_of(index * HD, HD), HD)

    def rows(index, base):
        return pl.ds(pl.multiple_of(base + index * HD, HD), HD)

    streams = ((k_ref, k_buf, WIN), (v_ref, v_buf, WIN), (q_ref, q_buf, 0))
    early = [
        pltpu.make_async_copy(gu_ref.at[0, 0], gu_buf, local_sem.at[0]),
        pltpu.make_async_copy(down_ref.at[0, 0], down_buf, local_sem.at[1]),
    ]
    local = [
        pltpu.make_async_copy(src.at[0, :, block(h)], dst.at[rows(h, base)], local_sem.at[2 + n])
        for n, (src, dst, base) in enumerate(streams)
    ]
    local += [
        pltpu.make_async_copy(src, dst, local_sem.at[5 + n])
        for n, (src, dst) in enumerate(
            (
                (fresh_gu_ref.at[0], fgu_buf),
                (fresh_down_ref.at[0], fdown_buf),
                (rates_ref.at[0], rate_ref),
                (gains_ref, gain_ref),
                (seqs_ref, seq_ref),
                (lens_ref, len_ref),
            )
        )
    ]
    for copy in early + local:
        copy.start()
    for copy in early:
        copy.wait()

    def encode(matrix, code, row):
        largest = jnp.maximum(jnp.max(jnp.abs(matrix), axis=0, keepdims=True), 1e-30)
        code[...] = jnp.round(matrix * (STEPS / largest)).astype(jnp.int32).astype(jnp.int16)
        scale_code[row : row + 1, : matrix.shape[1]] = largest * (1.0 / STEPS)

    def decode(code, row):
        return code.astype(jnp.int32).astype(jnp.float32) * scale_in[row : row + 1, : code.shape[1]]

    scale_code[...] = jnp.zeros_like(scale_code)
    encode(gu_buf[0], gu_code.at[0], 0)
    encode(gu_buf[1], gu_code.at[1], 1)
    encode(down_buf[...], down_code, 2)

    pl.semaphore_wait(barrier, n_peer + 1)

    receives = {}
    token_sends, ctx_sends = [], []

    def remote(name, group, src, dst, there, sem, here):
        def describe(at):
            return pltpu.make_async_remote_copy(
                src_ref=src, dst_ref=at, send_sem=send_sem.at[sem], recv_sem=recv_sem.at[sem],
                device_id=there, device_id_type=MESH,
            )

        group.append(describe(dst))
        receives.setdefault(name, []).append(describe(here))

    sem = 0
    for n, (src, dst, base) in enumerate(streams):
        for out, back in zip(to_peer, from_peer):
            remote(
                "tokens", token_sends, src.at[0, :, block(out)], dst.at[rows(h, base)], (c, out), sem,
                dst.at[rows(back, base)],
            )
            sem += 1
    recent, older = pl.ds(WIN // 2, WIN // 2), pl.ds(0, WIN // 2)
    for name, src, dst in (
        ("state", scale_code, scale_in),
        ("state", gu_code, gu_in),
        ("state", down_code, down_in),
        ("recent", tail_k_ref.at[recent], k_buf.at[recent]),
        ("recent", tail_v_ref.at[recent], v_buf.at[recent]),
        ("older", tail_k_ref.at[older], k_buf.at[older]),
        ("older", tail_v_ref.at[older], v_buf.at[older]),
    ):
        remote(name, ctx_sends, src, dst, (succ, h), sem, dst)
        sem += 1
    sends = token_sends + ctx_sends

    for copy in sends:
        copy.start()

    for copy in local:
        copy.wait()
    length = len_ref[0, c]
    linked = (seq_ref[1, c] == seq_ref[0, pred]).astype(jnp.int32)
    gain = gain_ref[...]
    exponent_scale = math.log2(math.e) / math.sqrt(HD)

    def attend(start):
        cols = WIN + TILE
        scores = nt(q_buf[pl.ds(start, TILE)], k_buf[pl.ds(start, cols)])
        key_pos = start - WIN + lax.broadcasted_iota(jnp.int32, (1, cols), 1)
        usable = jnp.where(key_pos < length, 1, 0) * jnp.where(key_pos >= 0, 1, linked)
        bias = jnp.where(usable > 0, 0.0, NEG)
        row = lax.broadcasted_iota(jnp.int32, (TILE, TILE), 0)
        col = lax.broadcasted_iota(jnp.int32, (TILE, TILE), 1)
        pieces = []
        for at in range(0, cols, TILE):
            own = scores[:, at : at + TILE]
            masked = own + bias[:, at : at + TILE]
            if at == 0:
                masked = jnp.where(col > row, masked, NEG)
            elif at == WIN:
                masked = jnp.where(col < row, masked, jnp.where(col == row, own, NEG))
            pieces.append(masked)
        scores = jnp.concatenate(pieces, axis=1)
        largest = jnp.max(scores, axis=-1, keepdims=True)
        exponent = jnp.exp2((scores - largest) * exponent_scale)
        total = jnp.sum(exponent, axis=-1, keepdims=True)
        weights = (exponent * (1.0 / total)).astype(jnp.bfloat16)
        return nn(weights, v_buf[pl.ds(start, cols)])

    for copy in receives["tokens"]:
        copy.wait_recv()
    for start in range(WIN, BLOCK, TILE):
        part_buf[pl.ds(start, TILE)] = attend(start)

    for copy in receives["state"]:
        copy.wait_recv()
    w_gate = jnp.where(linked > 0, decode(gu_in[0], 0), fgu_buf[0])
    w_up = jnp.where(linked > 0, decode(gu_in[1], 1), fgu_buf[1])
    w_down = jnp.where(linked > 0, decode(down_in[...], 2), fdown_buf[...])
    down_high, down_low = split(w_down)
    gate_high, gate_low = split(w_gate)
    up_high, up_low = split(w_up)
    in_weights = jnp.concatenate(
        [
            jnp.concatenate([gate_high, up_high], axis=1),
            jnp.concatenate([gate_low, up_low], axis=1),
        ],
        axis=0,
    )
    out_weights = jnp.concatenate([down_high, down_low], axis=1)

    def fast(start):
        own = q_buf[pl.ds(start, TILE)]
        wide = own.astype(jnp.float32)
        unit = lax.rsqrt(jnp.mean(wide * wide, axis=-1, keepdims=True) + EPS)
        hidden = nn(jnp.concatenate([own, own], axis=1), in_weights) * unit
        gate, up = hidden[:, :HID], hidden[:, HID:]
        act_high, act_low = split(gate * sigmoid(gate) * up)
        both = nn(act_high, out_weights)
        result = both[:, :HD] + both[:, HD:] + nn(act_low, down_high)
        scale = lax.rsqrt(jnp.mean(result * result, axis=-1, keepdims=True) + EPS)
        return result * scale * gain

    def finish(start, value):
        live = (start + lax.broadcasted_iota(jnp.int32, (TILE, 1), 0)) < length
        out_buf[pl.ds(start, TILE)] = jnp.where(live, value, 0.0).astype(jnp.bfloat16)

    for start in range(WIN, BLOCK, TILE):
        finish(start, part_buf[pl.ds(start, TILE)] + fast(start))
    for start in range(0, WIN, TILE):
        part_buf[pl.ds(start, TILE)] = fast(start)

    out_receives = [
        pltpu.make_async_remote_copy(
            src_ref=out_buf.at[rows(out, 0)], dst_ref=mixed_ref.at[0, :, block(back)],
            send_sem=out_send_sem.at[n], recv_sem=out_recv_sem.at[n],
            device_id=(c, out), device_id_type=MESH,
        )
        for n, (out, back) in enumerate(zip(to_peer, from_peer))
    ]
    out_sends = [
        pltpu.make_async_remote_copy(
            src_ref=out_buf.at[rows(out, 0)], dst_ref=mixed_ref.at[0, :, block(h)],
            send_sem=out_send_sem.at[n], recv_sem=out_recv_sem.at[n],
            device_id=(c, out), device_id_type=MESH,
        )
        for n, out in enumerate(to_peer)
    ]
    own_part = pltpu.make_async_copy(
        out_buf.at[rows(h, 0)], mixed_ref.at[0, :, block(h)], local_sem.at[0]
    )

    def send_rows(start, stop):
        for copy, out in [*zip(out_sends, to_peer), (own_part, h)]:
            @pl.when((out >= start // HD) & (out < stop // HD))
            def _():
                copy.start()

    send_rows(WIN, BLOCK)

    for copy in receives["recent"]:
        copy.wait_recv()
    finish(TILE, part_buf[pl.ds(TILE, TILE)] + attend(TILE))
    send_rows(TILE, WIN)
    for copy in receives["older"]:
        copy.wait_recv()
    finish(0, part_buf[pl.ds(0, TILE)] + attend(0))
    send_rows(0, TILE)

    key_weights = jnp.concatenate(
        [
            jnp.concatenate(split(w_gate.T), axis=1),
            jnp.concatenate(split(w_up.T), axis=1),
        ],
        axis=0,
    )
    ones = jnp.ones((8, 2 * HD), jnp.bfloat16)
    grad_in = jnp.zeros((2 * HID, HD), jnp.float32)
    grad_down = jnp.zeros((HID, HD), jnp.float32)
    for start in range(0, BLOCK, TILE):
        key = k_buf[pl.ds(WIN + start, TILE)]
        value = v_buf[pl.ds(WIN + start, TILE)]
        wide = key.astype(jnp.float32)
        squares = nt(ones, jnp.concatenate(split(wide * wide), axis=1))[0:1]
        unit = lax.rsqrt(squares * (1.0 / HD) + EPS)
        token = start + lax.broadcasted_iota(jnp.int32, (1, TILE), 1)
        rate = jnp.where(token < length, rate_ref[:, pl.ds(start, TILE)], 0.0)
        hidden = nt(key_weights, jnp.concatenate([key, key], axis=1)) * unit
        gate, up = hidden[:HID], hidden[HID:]
        s = sigmoid(gate)
        act = gate * s
        back = nt(out_weights, jnp.concatenate([value, value], axis=1)) * rate
        grad_down += nn((act * up * rate).astype(jnp.bfloat16), value)
        back = back * unit
        factor = jnp.concatenate([back * up * s * (1.0 + gate * (1.0 - s)), back * act], axis=0)
        grad_in += nn(factor.astype(jnp.bfloat16), key)

    def renormed(old, new):
        old_mean = jnp.mean(old * old, axis=0, keepdims=True) + EPS
        new_mean = jnp.mean(new * new, axis=0, keepdims=True) + EPS
        return new * (jnp.sqrt(old_mean) * lax.rsqrt(new_mean))

    gu_out_ref[0, 0, 0] = renormed(w_gate, w_gate + grad_in[:HID].T)
    gu_out_ref[0, 0, 1] = renormed(w_up, w_up + grad_in[HID:].T)
    down_out_ref[0, 0] = renormed(w_down, w_down + grad_down)

    own_part.wait()
    for copy in sends + out_sends:
        copy.wait_send()
    for copy in out_receives:
        copy.wait_recv()


def solution(mesh):
    ctx_count = mesh.shape["ctx"]
    n_remote = 3 * len(PEERS) + 7

    def on_device(
        queries, keys, values, rates, tail_keys, tail_values, state_in_gu, state_in_down,
        fresh_gu, fresh_down, out_gain, seq_ids, live_lengths,
    ):
        hbm = pl.BlockSpec(memory_space=pltpu.HBM)
        vmem = pl.BlockSpec(memory_space=pltpu.VMEM)

        def body(*refs):
            kernel(ctx_count, *refs)

        results = pl.pallas_call(
            body,
            name="layer",
            out_shape=(
                jax.ShapeDtypeStruct(queries.shape, jnp.bfloat16),
                jax.ShapeDtypeStruct(state_in_gu.shape, jnp.float32),
                jax.ShapeDtypeStruct(state_in_down.shape, jnp.float32),
            ),
            in_specs=[hbm] * 13,
            out_specs=(vmem, vmem, vmem),
            scratch_shapes=[
                pltpu.VMEM((BLOCK, HD), jnp.bfloat16),
                pltpu.VMEM((WIN + BLOCK, HD), jnp.bfloat16),
                pltpu.VMEM((WIN + BLOCK, HD), jnp.bfloat16),
                pltpu.VMEM((2, HD, HID), jnp.float32),
                pltpu.VMEM((HID, HD), jnp.float32),
                pltpu.VMEM((2, HD, HID), jnp.float32),
                pltpu.VMEM((HID, HD), jnp.float32),
                pltpu.VMEM((BLOCK, HD), jnp.bfloat16),
                pltpu.VMEM((BLOCK, HD), jnp.float32),
                pltpu.VMEM((2, HD, HID), jnp.int16),
                pltpu.VMEM((HID, HD), jnp.int16),
                pltpu.VMEM((8, HID), jnp.float32),
                pltpu.VMEM((2, HD, HID), jnp.int16),
                pltpu.VMEM((HID, HD), jnp.int16),
                pltpu.VMEM((8, HID), jnp.float32),
                pltpu.VMEM((1, BLOCK), jnp.float32),
                pltpu.VMEM((1, HD), jnp.float32),
                pltpu.SMEM((2, ctx_count), jnp.int32),
                pltpu.SMEM((1, ctx_count), jnp.int32),
                pltpu.SemaphoreType.DMA((11,)),
                pltpu.SemaphoreType.DMA((n_remote,)),
                pltpu.SemaphoreType.DMA((n_remote,)),
                pltpu.SemaphoreType.DMA((len(PEERS),)),
                pltpu.SemaphoreType.DMA((len(PEERS),)),
            ],
            compiler_params=pltpu.CompilerParams(
                collective_id=0, has_side_effects=True, vmem_limit_bytes=40 * 1024 * 1024
            ),
        )(
            *[
                pltpu.with_memory_space_constraint(array, pltpu.HBM)
                for array in (
                    queries, keys, values, rates, tail_keys, tail_values, state_in_gu, state_in_down,
                    fresh_gu, fresh_down, out_gain[None], seq_ids.T, live_lengths.T,
                )
            ]
        )

        def store(*refs):
            copies = [
                pltpu.make_async_copy(refs[n], refs[n + 3], refs[6].at[n]) for n in range(3)
            ]
            for copy in copies:
                copy.start()
            for copy in copies:
                copy.wait()

        return pl.pallas_call(
            store,
            name="store",
            out_shape=tuple(jax.ShapeDtypeStruct(r.shape, r.dtype) for r in results),
            in_specs=[vmem] * 3,
            out_specs=[hbm] * 3,
            scratch_shapes=[pltpu.SemaphoreType.DMA((3,))],
            compiler_params=pltpu.CompilerParams(vmem_limit_bytes=8 * 1024 * 1024),
        )(*results)

    placed = (
        P(None, ("ctx", "head"), None),
        P(None, ("ctx", "head"), None),
        P(None, ("ctx", "head"), None),
        P(None, "head", "ctx"),
        P("ctx", "head"),
        P("ctx", "head"),
        P("ctx", "head", None, None, None),
        P("ctx", "head", None, None),
        P("head", None, None, None),
        P("head", None, None),
        P("head"),
        P(),
        P(),
    )
    return jax.shard_map(
        on_device,
        mesh=mesh,
        in_specs=placed,
        out_specs=(
            P(None, ("ctx", "head"), None),
            P("ctx", "head", None, None, None),
            P("ctx", "head", None, None),
        ),
        check_vma=False,
    )
```

```python
import math

import jax
import jax.numpy as jnp
from jax import lax
from jax.experimental import pallas as pl
from jax.experimental.pallas import tpu as pltpu
from jax.sharding import PartitionSpec as P

MESH = pl.DeviceIdType.MESH
EPS = 1e-06
NEG = -1e30
HD = 128
HID = 256
BLOCK = 1024
WIN = 512
TILE = 256
X_SIZE = 4
Z_SIZE = 2
ROW = 8
STEPS = 32767.0
PEERS = tuple((dx, dz) for dz in (1, 0) for dx in (2, 1, 3, 0) if (dx, dz) != (0, 0))


def nt(left, right):
    return lax.dot_general(left, right, (((1,), (1,)), ((), ())), preferred_element_type=jnp.float32)


def nn(left, right):
    return jnp.dot(left, right, preferred_element_type=jnp.float32)


def split(matrix):
    high = matrix.astype(jnp.bfloat16)
    low = (matrix - high.astype(jnp.float32)).astype(jnp.bfloat16)
    return high, low


def sigmoid(x):
    return 0.5 * jnp.tanh(0.5 * x) + 0.5


def kernel(
    ctx_count,
    q_ref, k_ref, v_ref, rates_ref, tail_k_ref, tail_v_ref, gu_ref, down_ref,
    fresh_gu_ref, fresh_down_ref, gains_ref, seqs_ref, lens_ref,
    mixed_ref, gu_out_ref, down_out_ref,
    q_buf, k_buf, v_buf, gu_buf, down_buf, fgu_buf, fdown_buf, out_buf, part_buf,
    gu_code, down_code, scale_code, gu_in, down_in, scale_in,
    rate_ref, gain_ref, seq_ref, len_ref, relay_buf,
    local_sem, send_sem, recv_sem, out_send_sem, out_recv_sem, relay_send_sem, relay_recv_sem,
):
    c = lax.axis_index("ctx")
    h = lax.axis_index("head")
    succ = lax.rem(c + 1, ctx_count)
    pred = lax.rem(c + ctx_count - 1, ctx_count)
    hx, hz = h // Z_SIZE, lax.rem(h, Z_SIZE)
    to_peer = [
        lax.rem(hx + dx, X_SIZE) * Z_SIZE + lax.rem(hz + dz, Z_SIZE) for dx, dz in PEERS
    ]
    from_peer = [
        lax.rem(hx + X_SIZE - dx, X_SIZE) * Z_SIZE + lax.rem(hz + dz, Z_SIZE) for dx, dz in PEERS
    ]
    n_peer = len(PEERS)

    barrier = pltpu.get_barrier_semaphore()
    for peer in to_peer:
        pl.semaphore_signal(barrier, inc=1, device_id=(c, peer), device_id_type=MESH)
    pl.semaphore_signal(barrier, inc=1, device_id=(pred, h), device_id_type=MESH)
    at_row = lax.rem(c, ROW)
    row = c - at_row
    origin = (at_row == ROW - 1) & (hz == 0)
    middle = (at_row == 3) & (hz == 1)
    final = (at_row == 0) & (hz == 0)
    middle_id = (row + 3, h + 1)
    final_id = (lax.rem(row + ROW, ctx_count), h - 1)

    @pl.when(final)
    def _():
        there = (lax.rem(row + ctx_count - ROW, ctx_count) + 3, h + 1)
        pl.semaphore_signal(barrier, inc=1, device_id=there, device_id_type=MESH)

    @pl.when(middle)
    def _():
        there = (row + ROW - 1, h - 1)
        pl.semaphore_signal(barrier, inc=1, device_id=there, device_id_type=MESH)


    def block(index):
        return pl.ds(pl.multiple_of(index * HD, HD), HD)

    def rows(index, base):
        return pl.ds(pl.multiple_of(base + index * HD, HD), HD)

    streams = ((k_ref, k_buf, WIN), (v_ref, v_buf, WIN), (q_ref, q_buf, 0))
    early = [
        pltpu.make_async_copy(gu_ref.at[0, 0], gu_buf, local_sem.at[0]),
        pltpu.make_async_copy(down_ref.at[0, 0], down_buf, local_sem.at[1]),
    ]
    local = [
        pltpu.make_async_copy(src.at[0, :, block(h)], dst.at[rows(h, base)], local_sem.at[2 + n])
        for n, (src, dst, base) in enumerate(streams)
    ]
    local += [
        pltpu.make_async_copy(src, dst, local_sem.at[5 + n])
        for n, (src, dst) in enumerate(
            (
                (fresh_gu_ref.at[0], fgu_buf),
                (fresh_down_ref.at[0], fdown_buf),
                (rates_ref.at[0], rate_ref),
                (gains_ref, gain_ref),
                (seqs_ref, seq_ref),
                (lens_ref, len_ref),
            )
        )
    ]
    for copy in early + local:
        copy.start()
    for copy in early:
        copy.wait()

    def encode(matrix, code, row):
        largest = jnp.maximum(jnp.max(jnp.abs(matrix), axis=0, keepdims=True), 1e-30)
        code[...] = jnp.round(matrix * (STEPS / largest)).astype(jnp.int32).astype(jnp.int16)
        scale_code[row : row + 1, : matrix.shape[1]] = largest * (1.0 / STEPS)

    def decode(code, row):
        return code.astype(jnp.int32).astype(jnp.float32) * scale_in[row : row + 1, : code.shape[1]]

    scale_code[...] = jnp.zeros_like(scale_code)
    encode(gu_buf[0], gu_code.at[0], 0)
    encode(gu_buf[1], gu_code.at[1], 1)
    encode(down_buf[...], down_code, 2)

    @pl.when(origin | middle)
    def _():
        pl.semaphore_wait(barrier, n_peer + 2)

    @pl.when(jnp.logical_not(origin | middle))
    def _():
        pl.semaphore_wait(barrier, n_peer + 1)


    receives = {}
    token_sends, ctx_sends = [], []

    def remote(name, group, src, dst, there, sem, here):
        def describe(at):
            return pltpu.make_async_remote_copy(
                src_ref=src, dst_ref=at, send_sem=send_sem.at[sem], recv_sem=recv_sem.at[sem],
                device_id=there, device_id_type=MESH,
            )

        group.append(describe(dst))
        receives.setdefault(name, []).append(describe(here))

    sem = 0
    for n, (src, dst, base) in enumerate(streams):
        for out, back in zip(to_peer, from_peer):
            remote(
                "tokens", token_sends, src.at[0, :, block(out)], dst.at[rows(h, base)], (c, out), sem,
                dst.at[rows(back, base)],
            )
            sem += 1
    recent, older = pl.ds(WIN // 2, WIN // 2), pl.ds(0, WIN // 2)
    for name, src, dst in (
        ("state", scale_code, scale_in),
        ("state", gu_code, gu_in),
        ("state", down_code, down_in),
        ("recent", tail_k_ref.at[recent], k_buf.at[recent]),
        ("recent", tail_v_ref.at[recent], v_buf.at[recent]),
        ("older", tail_k_ref.at[older], k_buf.at[older]),
        ("older", tail_v_ref.at[older], v_buf.at[older]),
    ):
        remote(name, ctx_sends, src, dst, (succ, h), sem, dst)
        sem += 1
    sends = token_sends + ctx_sends
    tail_sends = ctx_sends[3:]
    detours, forwards = [], []
    for n, (src, dst) in enumerate(
        (
            (tail_k_ref.at[recent], k_buf.at[recent]),
            (tail_v_ref.at[recent], v_buf.at[recent]),
            (tail_k_ref.at[older], k_buf.at[older]),
            (tail_v_ref.at[older], v_buf.at[older]),
        )
    ):
        at = sem - 4 + n
        detours.append(
            pltpu.make_async_remote_copy(
                src_ref=src, dst_ref=relay_buf.at[n], send_sem=send_sem.at[at],
                recv_sem=relay_recv_sem.at[n], device_id=middle_id, device_id_type=MESH,
            )
        )
        forwards.append(
            pltpu.make_async_remote_copy(
                src_ref=relay_buf.at[n], dst_ref=dst, send_sem=relay_send_sem.at[n],
                recv_sem=recv_sem.at[at], device_id=final_id, device_id_type=MESH,
            )
        )

    @pl.when(origin)
    def _():
        for copy in detours:
            copy.start()

    for copy in token_sends + ctx_sends[:3]:
        copy.start()

    @pl.when(jnp.logical_not(origin))
    def _():
        for copy in tail_sends:
            copy.start()

    @pl.when(middle)
    def _():
        for arriving, copy in zip(detours, forwards):
            arriving.wait_recv()
            copy.start()

    for copy in local:
        copy.wait()
    length = len_ref[0, c]
    linked = (seq_ref[1, c] == seq_ref[0, pred]).astype(jnp.int32)
    gain = gain_ref[...]
    exponent_scale = math.log2(math.e) / math.sqrt(HD)

    def attend(start):
        cols = WIN + TILE
        scores = nt(q_buf[pl.ds(start, TILE)], k_buf[pl.ds(start, cols)])
        key_pos = start - WIN + lax.broadcasted_iota(jnp.int32, (1, cols), 1)
        usable = jnp.where(key_pos < length, 1, 0) * jnp.where(key_pos >= 0, 1, linked)
        bias = jnp.where(usable > 0, 0.0, NEG)
        row = lax.broadcasted_iota(jnp.int32, (TILE, TILE), 0)
        col = lax.broadcasted_iota(jnp.int32, (TILE, TILE), 1)
        pieces = []
        for at in range(0, cols, TILE):
            own = scores[:, at : at + TILE]
            masked = own + bias[:, at : at + TILE]
            if at == 0:
                masked = jnp.where(col > row, masked, NEG)
            elif at == WIN:
                masked = jnp.where(col < row, masked, jnp.where(col == row, own, NEG))
            pieces.append(masked)
        scores = jnp.concatenate(pieces, axis=1)
        largest = jnp.max(scores, axis=-1, keepdims=True)
        exponent = jnp.exp2((scores - largest) * exponent_scale)
        total = jnp.sum(exponent, axis=-1, keepdims=True)
        weights = (exponent * (1.0 / total)).astype(jnp.bfloat16)
        return nn(weights, v_buf[pl.ds(start, cols)])

    for copy in receives["tokens"]:
        copy.wait_recv()
    for start in range(WIN, BLOCK, TILE):
        part_buf[pl.ds(start, TILE)] = attend(start)

    for copy in receives["state"]:
        copy.wait_recv()
    w_gate = jnp.where(linked > 0, decode(gu_in[0], 0), fgu_buf[0])
    w_up = jnp.where(linked > 0, decode(gu_in[1], 1), fgu_buf[1])
    w_down = jnp.where(linked > 0, decode(down_in[...], 2), fdown_buf[...])
    down_high, down_low = split(w_down)
    gate_high, gate_low = split(w_gate)
    up_high, up_low = split(w_up)
    in_weights = jnp.concatenate(
        [
            jnp.concatenate([gate_high, up_high], axis=1),
            jnp.concatenate([gate_low, up_low], axis=1),
        ],
        axis=0,
    )
    out_weights = jnp.concatenate([down_high, down_low], axis=1)

    def fast(start):
        own = q_buf[pl.ds(start, TILE)]
        wide = own.astype(jnp.float32)
        unit = lax.rsqrt(jnp.mean(wide * wide, axis=-1, keepdims=True) + EPS)
        hidden = nn(jnp.concatenate([own, own], axis=1), in_weights) * unit
        gate, up = hidden[:, :HID], hidden[:, HID:]
        act_high, act_low = split(gate * sigmoid(gate) * up)
        both = nn(act_high, out_weights)
        result = both[:, :HD] + both[:, HD:] + nn(act_low, down_high)
        scale = lax.rsqrt(jnp.mean(result * result, axis=-1, keepdims=True) + EPS)
        return result * scale * gain

    def finish(start, value):
        live = (start + lax.broadcasted_iota(jnp.int32, (TILE, 1), 0)) < length
        out_buf[pl.ds(start, TILE)] = jnp.where(live, value, 0.0).astype(jnp.bfloat16)

    for start in range(WIN, BLOCK, TILE):
        finish(start, part_buf[pl.ds(start, TILE)] + fast(start))
    for start in range(0, WIN, TILE):
        part_buf[pl.ds(start, TILE)] = fast(start)

    out_receives = [
        pltpu.make_async_remote_copy(
            src_ref=out_buf.at[rows(out, 0)], dst_ref=mixed_ref.at[0, :, block(back)],
            send_sem=out_send_sem.at[n], recv_sem=out_recv_sem.at[n],
            device_id=(c, out), device_id_type=MESH,
        )
        for n, (out, back) in enumerate(zip(to_peer, from_peer))
    ]
    out_sends = [
        pltpu.make_async_remote_copy(
            src_ref=out_buf.at[rows(out, 0)], dst_ref=mixed_ref.at[0, :, block(h)],
            send_sem=out_send_sem.at[n], recv_sem=out_recv_sem.at[n],
            device_id=(c, out), device_id_type=MESH,
        )
        for n, out in enumerate(to_peer)
    ]
    own_part = pltpu.make_async_copy(
        out_buf.at[rows(h, 0)], mixed_ref.at[0, :, block(h)], local_sem.at[0]
    )

    def send_rows(start, stop):
        for copy, out in [*zip(out_sends, to_peer), (own_part, h)]:
            @pl.when((out >= start // HD) & (out < stop // HD))
            def _():
                copy.start()

    send_rows(WIN, BLOCK)

    for copy in receives["recent"]:
        copy.wait_recv()
    finish(TILE, part_buf[pl.ds(TILE, TILE)] + attend(TILE))
    send_rows(TILE, WIN)
    for copy in receives["older"]:
        copy.wait_recv()
    finish(0, part_buf[pl.ds(0, TILE)] + attend(0))
    send_rows(0, TILE)

    key_weights = jnp.concatenate(
        [
            jnp.concatenate(split(w_gate.T), axis=1),
            jnp.concatenate(split(w_up.T), axis=1),
        ],
        axis=0,
    )
    ones = jnp.ones((8, 2 * HD), jnp.bfloat16)
    grad_in = jnp.zeros((2 * HID, HD), jnp.float32)
    grad_down = jnp.zeros((HID, HD), jnp.float32)
    for start in range(0, BLOCK, TILE):
        key = k_buf[pl.ds(WIN + start, TILE)]
        value = v_buf[pl.ds(WIN + start, TILE)]
        wide = key.astype(jnp.float32)
        squares = nt(ones, jnp.concatenate(split(wide * wide), axis=1))[0:1]
        unit = lax.rsqrt(squares * (1.0 / HD) + EPS)
        token = start + lax.broadcasted_iota(jnp.int32, (1, TILE), 1)
        rate = jnp.where(token < length, rate_ref[:, pl.ds(start, TILE)], 0.0)
        hidden = nt(key_weights, jnp.concatenate([key, key], axis=1)) * unit
        gate, up = hidden[:HID], hidden[HID:]
        s = sigmoid(gate)
        act = gate * s
        back = nt(out_weights, jnp.concatenate([value, value], axis=1)) * rate
        grad_down += nn((act * up * rate).astype(jnp.bfloat16), value)
        back = back * unit
        factor = jnp.concatenate([back * up * s * (1.0 + gate * (1.0 - s)), back * act], axis=0)
        grad_in += nn(factor.astype(jnp.bfloat16), key)

    def renormed(old, new):
        old_mean = jnp.mean(old * old, axis=0, keepdims=True) + EPS
        new_mean = jnp.mean(new * new, axis=0, keepdims=True) + EPS
        return new * (jnp.sqrt(old_mean) * lax.rsqrt(new_mean))

    gu_out_ref[0, 0, 0] = renormed(w_gate, w_gate + grad_in[:HID].T)
    gu_out_ref[0, 0, 1] = renormed(w_up, w_up + grad_in[HID:].T)
    down_out_ref[0, 0] = renormed(w_down, w_down + grad_down)

    own_part.wait()

    @pl.when(middle)
    def _():
        for copy in forwards:
            copy.wait_send()

    for copy in sends + out_sends:
        copy.wait_send()
    for copy in out_receives:
        copy.wait_recv()


def solution(mesh):
    ctx_count = mesh.shape["ctx"]
    n_remote = 3 * len(PEERS) + 7

    def on_device(
        queries, keys, values, rates, tail_keys, tail_values, state_in_gu, state_in_down,
        fresh_gu, fresh_down, out_gain, seq_ids, live_lengths,
    ):
        hbm = pl.BlockSpec(memory_space=pltpu.HBM)
        vmem = pl.BlockSpec(memory_space=pltpu.VMEM)

        def body(*refs):
            kernel(ctx_count, *refs)

        results = pl.pallas_call(
            body,
            name="layer",
            out_shape=(
                jax.ShapeDtypeStruct(queries.shape, jnp.bfloat16),
                jax.ShapeDtypeStruct(state_in_gu.shape, jnp.float32),
                jax.ShapeDtypeStruct(state_in_down.shape, jnp.float32),
            ),
            in_specs=[hbm] * 13,
            out_specs=(vmem, vmem, vmem),
            scratch_shapes=[
                pltpu.VMEM((BLOCK, HD), jnp.bfloat16),
                pltpu.VMEM((WIN + BLOCK, HD), jnp.bfloat16),
                pltpu.VMEM((WIN + BLOCK, HD), jnp.bfloat16),
                pltpu.VMEM((2, HD, HID), jnp.float32),
                pltpu.VMEM((HID, HD), jnp.float32),
                pltpu.VMEM((2, HD, HID), jnp.float32),
                pltpu.VMEM((HID, HD), jnp.float32),
                pltpu.VMEM((BLOCK, HD), jnp.bfloat16),
                pltpu.VMEM((BLOCK, HD), jnp.float32),
                pltpu.VMEM((2, HD, HID), jnp.int16),
                pltpu.VMEM((HID, HD), jnp.int16),
                pltpu.VMEM((8, HID), jnp.float32),
                pltpu.VMEM((2, HD, HID), jnp.int16),
                pltpu.VMEM((HID, HD), jnp.int16),
                pltpu.VMEM((8, HID), jnp.float32),
                pltpu.VMEM((1, BLOCK), jnp.float32),
                pltpu.VMEM((1, HD), jnp.float32),
                pltpu.SMEM((2, ctx_count), jnp.int32),
                pltpu.SMEM((1, ctx_count), jnp.int32),
                pltpu.VMEM((4, WIN // 2, HD), jnp.bfloat16),
                pltpu.SemaphoreType.DMA((11,)),
                pltpu.SemaphoreType.DMA((n_remote,)),
                pltpu.SemaphoreType.DMA((n_remote,)),
                pltpu.SemaphoreType.DMA((len(PEERS),)),
                pltpu.SemaphoreType.DMA((len(PEERS),)),
                pltpu.SemaphoreType.DMA((4,)),
                pltpu.SemaphoreType.DMA((4,)),
            ],
            compiler_params=pltpu.CompilerParams(
                collective_id=0, has_side_effects=True, vmem_limit_bytes=40 * 1024 * 1024
            ),
        )(
            *[
                pltpu.with_memory_space_constraint(array, pltpu.HBM)
                for array in (
                    queries, keys, values, rates, tail_keys, tail_values, state_in_gu, state_in_down,
                    fresh_gu, fresh_down, out_gain[None], seq_ids.T, live_lengths.T,
                )
            ]
        )

        def store(*refs):
            copies = [
                pltpu.make_async_copy(refs[n], refs[n + 3], refs[6].at[n]) for n in range(3)
            ]
            for copy in copies:
                copy.start()
            for copy in copies:
                copy.wait()

        return pl.pallas_call(
            store,
            name="store",
            out_shape=tuple(jax.ShapeDtypeStruct(r.shape, r.dtype) for r in results),
            in_specs=[vmem] * 3,
            out_specs=[hbm] * 3,
            scratch_shapes=[pltpu.SemaphoreType.DMA((3,))],
            compiler_params=pltpu.CompilerParams(vmem_limit_bytes=8 * 1024 * 1024),
        )(*results)

    placed = (
        P(None, ("ctx", "head"), None),
        P(None, ("ctx", "head"), None),
        P(None, ("ctx", "head"), None),
        P(None, "head", "ctx"),
        P("ctx", "head"),
        P("ctx", "head"),
        P("ctx", "head", None, None, None),
        P("ctx", "head", None, None),
        P("head", None, None, None),
        P("head", None, None),
        P("head"),
        P(),
        P(),
    )
    return jax.shard_map(
        on_device,
        mesh=mesh,
        in_specs=placed,
        out_specs=(
            P(None, ("ctx", "head"), None),
            P("ctx", "head", None, None, None),
            P("ctx", "head", None, None),
        ),
        check_vma=False,
    )
```

```python
import math

import jax
import jax.numpy as jnp
from jax import lax
from jax.experimental import pallas as pl
from jax.experimental.pallas import tpu as pltpu
from jax.sharding import PartitionSpec as P

MESH = pl.DeviceIdType.MESH
EPS = 1e-06
NEG = -1e30
HD = 128
HID = 256
BLOCK = 1024
WIN = 512
TILE = 256
X_SIZE = 4
Z_SIZE = 2
PLAN = (2, 1, 2, 1, 1, 1, 0, 0)
ROW = 8
STEPS = 32767.0
PEERS = tuple((dx, dz) for dz in (1, 0) for dx in (2, 1, 3, 0) if (dx, dz) != (0, 0))


def nt(left, right):
    return lax.dot_general(left, right, (((1,), (1,)), ((), ())), preferred_element_type=jnp.float32)


def nn(left, right):
    return jnp.dot(left, right, preferred_element_type=jnp.float32)


def split(matrix):
    high = matrix.astype(jnp.bfloat16)
    low = (matrix - high.astype(jnp.float32)).astype(jnp.bfloat16)
    return high, low


def sigmoid(x):
    return 0.5 * jnp.tanh(0.5 * x) + 0.5


def kernel(
    ctx_count,
    q_ref, k_ref, v_ref, rates_ref, tail_k_ref, tail_v_ref, gu_ref, down_ref,
    fresh_gu_ref, fresh_down_ref, gains_ref, seqs_ref, lens_ref,
    mixed_ref, gu_out_ref, down_out_ref,
    q_buf, k_buf, v_buf, gu_buf, down_buf, fgu_buf, fdown_buf, out_buf, part_buf,
    gu_code, down_code, scale_code, gu_in, down_in, scale_in,
    rate_ref, gain_ref, seq_ref, len_ref, relay_buf,
    local_sem, send_sem, recv_sem, out_send_sem, out_recv_sem, relay_send_sem, relay_recv_sem,
):
    c = lax.axis_index("ctx")
    h = lax.axis_index("head")
    succ = lax.rem(c + 1, ctx_count)
    pred = lax.rem(c + ctx_count - 1, ctx_count)
    hx, hz = h // Z_SIZE, lax.rem(h, Z_SIZE)
    to_peer = [
        lax.rem(hx + dx, X_SIZE) * Z_SIZE + lax.rem(hz + dz, Z_SIZE) for dx, dz in PEERS
    ]
    from_peer = [
        lax.rem(hx + X_SIZE - dx, X_SIZE) * Z_SIZE + lax.rem(hz + dz, Z_SIZE) for dx, dz in PEERS
    ]
    n_peer = len(PEERS)

    barrier = pltpu.get_barrier_semaphore()
    for peer in to_peer:
        pl.semaphore_signal(barrier, inc=1, device_id=(c, peer), device_id_type=MESH)
    pl.semaphore_signal(barrier, inc=1, device_id=(pred, h), device_id_type=MESH)
    at_row = lax.rem(c, ROW)
    row = c - at_row
    origin = (at_row == ROW - 1) & (hz == 0)
    middle = (at_row == 3) & (hz == 1)
    final = (at_row == 0) & (hz == 0)
    middle_id = (row + 3, h + 1)
    final_id = (lax.rem(row + ROW, ctx_count), h - 1)

    @pl.when(final)
    def _():
        there = (lax.rem(row + ctx_count - ROW, ctx_count) + 3, h + 1)
        pl.semaphore_signal(barrier, inc=1, device_id=there, device_id_type=MESH)

    @pl.when(middle)
    def _():
        there = (row + ROW - 1, h - 1)
        pl.semaphore_signal(barrier, inc=1, device_id=there, device_id_type=MESH)


    def block(index):
        return pl.ds(pl.multiple_of(index * HD, HD), HD)

    def rows(index, base):
        return pl.ds(pl.multiple_of(base + index * HD, HD), HD)

    streams = ((k_ref, k_buf, WIN), (v_ref, v_buf, WIN), (q_ref, q_buf, 0))
    early = [
        pltpu.make_async_copy(gu_ref.at[0, 0], gu_buf, local_sem.at[0]),
        pltpu.make_async_copy(down_ref.at[0, 0], down_buf, local_sem.at[1]),
    ]
    local = [
        pltpu.make_async_copy(src.at[0, :, block(h)], dst.at[rows(h, base)], local_sem.at[2 + n])
        for n, (src, dst, base) in enumerate(streams)
    ]
    local += [
        pltpu.make_async_copy(src, dst, local_sem.at[5 + n])
        for n, (src, dst) in enumerate(
            (
                (fresh_gu_ref.at[0], fgu_buf),
                (fresh_down_ref.at[0], fdown_buf),
                (rates_ref.at[0], rate_ref),
                (gains_ref, gain_ref),
                (seqs_ref, seq_ref),
                (lens_ref, len_ref),
            )
        )
    ]
    for copy in early + local:
        copy.start()
    for copy in early:
        copy.wait()

    def encode(matrix, code, row):
        largest = jnp.maximum(jnp.max(jnp.abs(matrix), axis=0, keepdims=True), 1e-30)
        code[...] = jnp.round(matrix * (STEPS / largest)).astype(jnp.int32).astype(jnp.int16)
        scale_code[row : row + 1, : matrix.shape[1]] = largest * (1.0 / STEPS)

    def decode(code, row):
        return code.astype(jnp.int32).astype(jnp.float32) * scale_in[row : row + 1, : code.shape[1]]

    scale_code[...] = jnp.zeros_like(scale_code)
    encode(gu_buf[0], gu_code.at[0], 0)
    encode(gu_buf[1], gu_code.at[1], 1)
    encode(down_buf[...], down_code, 2)

    @pl.when(origin | middle)
    def _():
        pl.semaphore_wait(barrier, n_peer + 2)

    @pl.when(jnp.logical_not(origin | middle))
    def _():
        pl.semaphore_wait(barrier, n_peer + 1)


    receives = {}
    token_sends, ctx_sends = [], []

    def remote(name, group, src, dst, there, sem, here):
        def describe(at):
            return pltpu.make_async_remote_copy(
                src_ref=src, dst_ref=at, send_sem=send_sem.at[sem], recv_sem=recv_sem.at[sem],
                device_id=there, device_id_type=MESH,
            )

        group.append(describe(dst))
        receives.setdefault(name, []).append(describe(here))

    sem = 0
    for dz in (1, 0):
        for src, dst, base in streams:
            for n in range(n_peer):
                if PEERS[n][1] == dz:
                    out, back = to_peer[n], from_peer[n]
                    remote(
                        "tokens", token_sends, src.at[0, :, block(out)], dst.at[rows(h, base)],
                        (c, out), sem, dst.at[rows(back, base)],
                    )
                    sem += 1
    recent, older = pl.ds(WIN // 2, WIN // 2), pl.ds(0, WIN // 2)
    for name, src, dst in (
        ("state", scale_code, scale_in),
        ("state", gu_code, gu_in),
        ("state", down_code, down_in),
        ("recent", tail_k_ref.at[recent], k_buf.at[recent]),
        ("recent", tail_v_ref.at[recent], v_buf.at[recent]),
        ("older", tail_k_ref.at[older], k_buf.at[older]),
        ("older", tail_v_ref.at[older], v_buf.at[older]),
    ):
        remote(name, ctx_sends, src, dst, (succ, h), sem, dst)
        sem += 1
    sends = token_sends[3 * X_SIZE :] + ctx_sends
    tail_sends = ctx_sends[3:]
    detours, forwards = [], []
    for n, (src, dst) in enumerate(
        (
            (tail_k_ref.at[recent], k_buf.at[recent]),
            (tail_v_ref.at[recent], v_buf.at[recent]),
            (tail_k_ref.at[older], k_buf.at[older]),
            (tail_v_ref.at[older], v_buf.at[older]),
        )
    ):
        at = sem - 4 + n
        detours.append(
            pltpu.make_async_remote_copy(
                src_ref=src, dst_ref=relay_buf.at[n], send_sem=send_sem.at[at],
                recv_sem=relay_recv_sem.at[n], device_id=middle_id, device_id_type=MESH,
            )
        )
        forwards.append(
            pltpu.make_async_remote_copy(
                src_ref=relay_buf.at[n], dst_ref=dst, send_sem=relay_send_sem.at[n],
                recv_sem=recv_sem.at[at], device_id=final_id, device_id_type=MESH,
            )
        )

    far = lax.rem(c, 2) == 1
    z = (at_row // 2) * Z_SIZE + hz

    def chosen(stage):
        picked = c < 0 if stage else jnp.logical_not(far)
        for at, planned in enumerate(PLAN):
            if planned == stage:
                picked = picked | ((z == at) & far)
        return picked

    def start_ctx(stage):
        when = chosen(stage)

        @pl.when(when)
        def _():
            for copy in ctx_sends[:3]:
                copy.start()

        @pl.when(when & jnp.logical_not(origin))
        def _():
            for copy in tail_sends:
                copy.start()

    crossing = token_sends[: 3 * X_SIZE]
    waits = chosen(2)

    def drain(when):
        @pl.when(when)
        def _():
            for copy in crossing:
                copy.wait_send()

    @pl.when(origin)
    def _():
        for copy in detours:
            copy.start()

    start_ctx(0)
    for copy in token_sends:
        copy.start()
    start_ctx(1)
    drain(waits)
    start_ctx(2)

    @pl.when(middle)
    def _():
        for arriving, copy in zip(detours, forwards):
            arriving.wait_recv()
            copy.start()

    for copy in local:
        copy.wait()
    length = len_ref[0, c]
    linked = (seq_ref[1, c] == seq_ref[0, pred]).astype(jnp.int32)
    gain = gain_ref[...]
    exponent_scale = math.log2(math.e) / math.sqrt(HD)

    def attend(start):
        cols = WIN + TILE
        scores = nt(q_buf[pl.ds(start, TILE)], k_buf[pl.ds(start, cols)])
        key_pos = start - WIN + lax.broadcasted_iota(jnp.int32, (1, cols), 1)
        usable = jnp.where(key_pos < length, 1, 0) * jnp.where(key_pos >= 0, 1, linked)
        bias = jnp.where(usable > 0, 0.0, NEG)
        row = lax.broadcasted_iota(jnp.int32, (TILE, TILE), 0)
        col = lax.broadcasted_iota(jnp.int32, (TILE, TILE), 1)
        pieces = []
        for at in range(0, cols, TILE):
            own = scores[:, at : at + TILE]
            masked = own + bias[:, at : at + TILE]
            if at == 0:
                masked = jnp.where(col > row, masked, NEG)
            elif at == WIN:
                masked = jnp.where(col < row, masked, jnp.where(col == row, own, NEG))
            pieces.append(masked)
        scores = jnp.concatenate(pieces, axis=1)
        largest = jnp.max(scores, axis=-1, keepdims=True)
        exponent = jnp.exp2((scores - largest) * exponent_scale)
        total = jnp.sum(exponent, axis=-1, keepdims=True)
        weights = (exponent * (1.0 / total)).astype(jnp.bfloat16)
        return nn(weights, v_buf[pl.ds(start, cols)])

    for copy in receives["tokens"]:
        copy.wait_recv()
    start_ctx(3)
    for start in range(WIN, BLOCK, TILE):
        part_buf[pl.ds(start, TILE)] = attend(start)

    for copy in receives["state"]:
        copy.wait_recv()
    w_gate = jnp.where(linked > 0, decode(gu_in[0], 0), fgu_buf[0])
    w_up = jnp.where(linked > 0, decode(gu_in[1], 1), fgu_buf[1])
    w_down = jnp.where(linked > 0, decode(down_in[...], 2), fdown_buf[...])
    down_high, down_low = split(w_down)
    gate_high, gate_low = split(w_gate)
    up_high, up_low = split(w_up)
    in_weights = jnp.concatenate(
        [
            jnp.concatenate([gate_high, up_high], axis=1),
            jnp.concatenate([gate_low, up_low], axis=1),
        ],
        axis=0,
    )
    out_weights = jnp.concatenate([down_high, down_low], axis=1)

    def fast(start):
        own = q_buf[pl.ds(start, TILE)]
        wide = own.astype(jnp.float32)
        unit = lax.rsqrt(jnp.mean(wide * wide, axis=-1, keepdims=True) + EPS)
        hidden = nn(jnp.concatenate([own, own], axis=1), in_weights) * unit
        gate, up = hidden[:, :HID], hidden[:, HID:]
        act_high, act_low = split(gate * sigmoid(gate) * up)
        both = nn(act_high, out_weights)
        result = both[:, :HD] + both[:, HD:] + nn(act_low, down_high)
        scale = lax.rsqrt(jnp.mean(result * result, axis=-1, keepdims=True) + EPS)
        return result * scale * gain

    def finish(start, value):
        live = (start + lax.broadcasted_iota(jnp.int32, (TILE, 1), 0)) < length
        out_buf[pl.ds(start, TILE)] = jnp.where(live, value, 0.0).astype(jnp.bfloat16)

    out_receives = [
        pltpu.make_async_remote_copy(
            src_ref=out_buf.at[rows(out, 0)], dst_ref=mixed_ref.at[0, :, block(back)],
            send_sem=out_send_sem.at[n], recv_sem=out_recv_sem.at[n],
            device_id=(c, out), device_id_type=MESH,
        )
        for n, (out, back) in enumerate(zip(to_peer, from_peer))
    ]
    out_sends = [
        pltpu.make_async_remote_copy(
            src_ref=out_buf.at[rows(out, 0)], dst_ref=mixed_ref.at[0, :, block(h)],
            send_sem=out_send_sem.at[n], recv_sem=out_recv_sem.at[n],
            device_id=(c, out), device_id_type=MESH,
        )
        for n, out in enumerate(to_peer)
    ]
    own_part = pltpu.make_async_copy(
        out_buf.at[rows(h, 0)], mixed_ref.at[0, :, block(h)], local_sem.at[0]
    )

    def send_rows(start, stop):
        for copy, out in [*zip(out_sends, to_peer), (own_part, h)]:
            @pl.when((out >= start // HD) & (out < stop // HD))
            def _():
                copy.start()

    def first_rows_fast():
        for start in range(0, WIN, TILE):
            part_buf[pl.ds(start, TILE)] = fast(start)

    def first_rows(start):
        finish(start, part_buf[pl.ds(start, TILE)] + attend(start))
        send_rows(start, start + TILE)

    def last_rows():
        for start in range(WIN, BLOCK, TILE):
            finish(start, part_buf[pl.ds(start, TILE)] + fast(start))
        send_rows(WIN, BLOCK)

    @pl.when(hz == 0)
    def _():
        last_rows()
        first_rows_fast()
        for copy in receives["recent"]:
            copy.wait_recv()
        first_rows(TILE)
        for copy in receives["older"]:
            copy.wait_recv()
        first_rows(0)

    @pl.when(hz != 0)
    def _():
        first_rows_fast()
        for copy in receives["recent"] + receives["older"]:
            copy.wait_recv()
        first_rows(0)
        first_rows(TILE)
        last_rows()

    key_weights = jnp.concatenate(
        [
            jnp.concatenate(split(w_gate.T), axis=1),
            jnp.concatenate(split(w_up.T), axis=1),
        ],
        axis=0,
    )
    ones = jnp.ones((8, 2 * HD), jnp.bfloat16)
    grad_in = jnp.zeros((2 * HID, HD), jnp.float32)
    grad_down = jnp.zeros((HID, HD), jnp.float32)
    for start in range(0, BLOCK, TILE):
        key = k_buf[pl.ds(WIN + start, TILE)]
        value = v_buf[pl.ds(WIN + start, TILE)]
        wide = key.astype(jnp.float32)
        squares = nt(ones, jnp.concatenate(split(wide * wide), axis=1))[0:1]
        unit = lax.rsqrt(squares * (1.0 / HD) + EPS)
        token = start + lax.broadcasted_iota(jnp.int32, (1, TILE), 1)
        rate = jnp.where(token < length, rate_ref[:, pl.ds(start, TILE)], 0.0)
        hidden = nt(key_weights, jnp.concatenate([key, key], axis=1)) * unit
        gate, up = hidden[:HID], hidden[HID:]
        s = sigmoid(gate)
        act = gate * s
        back = nt(out_weights, jnp.concatenate([value, value], axis=1)) * rate
        grad_down += nn((act * up * rate).astype(jnp.bfloat16), value)
        back = back * unit
        factor = jnp.concatenate([back * up * s * (1.0 + gate * (1.0 - s)), back * act], axis=0)
        grad_in += nn(factor.astype(jnp.bfloat16), key)

    def renormed(old, new):
        old_mean = jnp.mean(old * old, axis=0, keepdims=True) + EPS
        new_mean = jnp.mean(new * new, axis=0, keepdims=True) + EPS
        return new * (jnp.sqrt(old_mean) * lax.rsqrt(new_mean))

    gu_out_ref[0, 0, 0] = renormed(w_gate, w_gate + grad_in[:HID].T)
    gu_out_ref[0, 0, 1] = renormed(w_up, w_up + grad_in[HID:].T)
    down_out_ref[0, 0] = renormed(w_down, w_down + grad_down)

    own_part.wait()
    drain(jnp.logical_not(waits))

    @pl.when(middle)
    def _():
        for copy in forwards:
            copy.wait_send()

    for copy in sends + out_sends:
        copy.wait_send()
    for copy in out_receives:
        copy.wait_recv()


def solution(mesh):
    ctx_count = mesh.shape["ctx"]
    n_remote = 3 * len(PEERS) + 7

    def on_device(
        queries, keys, values, rates, tail_keys, tail_values, state_in_gu, state_in_down,
        fresh_gu, fresh_down, out_gain, seq_ids, live_lengths,
    ):
        hbm = pl.BlockSpec(memory_space=pltpu.HBM)
        vmem = pl.BlockSpec(memory_space=pltpu.VMEM)

        def body(*refs):
            kernel(ctx_count, *refs)

        results = pl.pallas_call(
            body,
            name="layer",
            out_shape=(
                jax.ShapeDtypeStruct(queries.shape, jnp.bfloat16),
                jax.ShapeDtypeStruct(state_in_gu.shape, jnp.float32),
                jax.ShapeDtypeStruct(state_in_down.shape, jnp.float32),
            ),
            in_specs=[hbm] * 13,
            out_specs=(vmem, vmem, vmem),
            scratch_shapes=[
                pltpu.VMEM((BLOCK, HD), jnp.bfloat16),
                pltpu.VMEM((WIN + BLOCK, HD), jnp.bfloat16),
                pltpu.VMEM((WIN + BLOCK, HD), jnp.bfloat16),
                pltpu.VMEM((2, HD, HID), jnp.float32),
                pltpu.VMEM((HID, HD), jnp.float32),
                pltpu.VMEM((2, HD, HID), jnp.float32),
                pltpu.VMEM((HID, HD), jnp.float32),
                pltpu.VMEM((BLOCK, HD), jnp.bfloat16),
                pltpu.VMEM((BLOCK, HD), jnp.float32),
                pltpu.VMEM((2, HD, HID), jnp.int16),
                pltpu.VMEM((HID, HD), jnp.int16),
                pltpu.VMEM((8, HID), jnp.float32),
                pltpu.VMEM((2, HD, HID), jnp.int16),
                pltpu.VMEM((HID, HD), jnp.int16),
                pltpu.VMEM((8, HID), jnp.float32),
                pltpu.VMEM((1, BLOCK), jnp.float32),
                pltpu.VMEM((1, HD), jnp.float32),
                pltpu.SMEM((2, ctx_count), jnp.int32),
                pltpu.SMEM((1, ctx_count), jnp.int32),
                pltpu.VMEM((4, WIN // 2, HD), jnp.bfloat16),
                pltpu.SemaphoreType.DMA((11,)),
                pltpu.SemaphoreType.DMA((n_remote,)),
                pltpu.SemaphoreType.DMA((n_remote,)),
                pltpu.SemaphoreType.DMA((len(PEERS),)),
                pltpu.SemaphoreType.DMA((len(PEERS),)),
                pltpu.SemaphoreType.DMA((4,)),
                pltpu.SemaphoreType.DMA((4,)),
            ],
            compiler_params=pltpu.CompilerParams(
                collective_id=0, has_side_effects=True, vmem_limit_bytes=40 * 1024 * 1024
            ),
        )(
            *[
                pltpu.with_memory_space_constraint(array, pltpu.HBM)
                for array in (
                    queries, keys, values, rates, tail_keys, tail_values, state_in_gu, state_in_down,
                    fresh_gu, fresh_down, out_gain[None], seq_ids.T, live_lengths.T,
                )
            ]
        )

        def store(*refs):
            copies = [
                pltpu.make_async_copy(refs[n], refs[n + 3], refs[6].at[n]) for n in range(3)
            ]
            for copy in copies:
                copy.start()
            for copy in copies:
                copy.wait()

        return pl.pallas_call(
            store,
            name="store",
            out_shape=tuple(jax.ShapeDtypeStruct(r.shape, r.dtype) for r in results),
            in_specs=[vmem] * 3,
            out_specs=[hbm] * 3,
            scratch_shapes=[pltpu.SemaphoreType.DMA((3,))],
            compiler_params=pltpu.CompilerParams(vmem_limit_bytes=8 * 1024 * 1024),
        )(*results)

    placed = (
        P(None, ("ctx", "head"), None),
        P(None, ("ctx", "head"), None),
        P(None, ("ctx", "head"), None),
        P(None, "head", "ctx"),
        P("ctx", "head"),
        P("ctx", "head"),
        P("ctx", "head", None, None, None),
        P("ctx", "head", None, None),
        P("head", None, None, None),
        P("head", None, None),
        P("head"),
        P(),
        P(),
    )
    return jax.shard_map(
        on_device,
        mesh=mesh,
        in_specs=placed,
        out_specs=(
            P(None, ("ctx", "head"), None),
            P("ctx", "head", None, None, None),
            P("ctx", "head", None, None),
        ),
        check_vma=False,
    )
```

```python
import math

import jax
import jax.numpy as jnp
from jax import lax
from jax.experimental import pallas as pl
from jax.experimental.pallas import tpu as pltpu
from jax.sharding import PartitionSpec as P

MESH = pl.DeviceIdType.MESH
EPS = 1e-06
NEG = -1e30
HD = 128
HID = 256
BLOCK = 1024
WIN = 512
TILE = 256
X_SIZE = 4
Z_SIZE = 2
PLAN = (2, 1, 2, 1, 1, 1, 0, 0)
ROW = 8
STEPS = 32767.0
PEERS = tuple((dx, dz) for dz in (1, 0) for dx in (2, 1, 3, 0) if (dx, dz) != (0, 0))


def nt(left, right):
    return lax.dot_general(left, right, (((1,), (1,)), ((), ())), preferred_element_type=jnp.float32)


def nn(left, right):
    return jnp.dot(left, right, preferred_element_type=jnp.float32)


def split(matrix):
    high = matrix.astype(jnp.bfloat16)
    low = (matrix - high.astype(jnp.float32)).astype(jnp.bfloat16)
    return high, low


def sigmoid(x):
    return 0.5 * jnp.tanh(0.5 * x) + 0.5


def kernel(
    ctx_count,
    q_ref, k_ref, v_ref, rates_ref, tail_k_ref, tail_v_ref, gu_ref, down_ref,
    fresh_gu_ref, fresh_down_ref, gains_ref, seqs_ref, lens_ref,
    mixed_ref, gu_out_ref, down_out_ref,
    q_buf, k_buf, v_buf, gu_buf, down_buf, fgu_buf, fdown_buf, out_buf, part_buf,
    gu_code, down_code, scale_code, gu_in, down_in, scale_in,
    rate_ref, gain_ref, seq_ref, len_ref, relay_buf,
    local_sem, send_sem, recv_sem, out_send_sem, out_recv_sem, relay_send_sem, relay_recv_sem,
):
    c = lax.axis_index("ctx")
    h = lax.axis_index("head")
    succ = lax.rem(c + 1, ctx_count)
    pred = lax.rem(c + ctx_count - 1, ctx_count)
    hx, hz = h // Z_SIZE, lax.rem(h, Z_SIZE)
    to_peer = [
        lax.rem(hx + dx, X_SIZE) * Z_SIZE + lax.rem(hz + dz, Z_SIZE) for dx, dz in PEERS
    ]
    from_peer = [
        lax.rem(hx + X_SIZE - dx, X_SIZE) * Z_SIZE + lax.rem(hz + dz, Z_SIZE) for dx, dz in PEERS
    ]
    n_peer = len(PEERS)

    barrier = pltpu.get_barrier_semaphore()
    for peer in to_peer:
        pl.semaphore_signal(barrier, inc=1, device_id=(c, peer), device_id_type=MESH)
    pl.semaphore_signal(barrier, inc=1, device_id=(pred, h), device_id_type=MESH)
    at_row = lax.rem(c, ROW)
    row = c - at_row
    origin = (at_row == ROW - 1) & (hz == 0)
    middle = (at_row == 3) & (hz == 1)
    final = (at_row == 0) & (hz == 0)
    middle_id = (row + 3, h + 1)
    final_id = (lax.rem(row + ROW, ctx_count), h - 1)

    @pl.when(final)
    def _():
        there = (lax.rem(row + ctx_count - ROW, ctx_count) + 3, h + 1)
        pl.semaphore_signal(barrier, inc=1, device_id=there, device_id_type=MESH)

    @pl.when(middle)
    def _():
        there = (row + ROW - 1, h - 1)
        pl.semaphore_signal(barrier, inc=1, device_id=there, device_id_type=MESH)


    def block(index):
        return pl.ds(pl.multiple_of(index * HD, HD), HD)

    def rows(index, base):
        return pl.ds(pl.multiple_of(base + index * HD, HD), HD)

    streams = ((k_ref, k_buf, WIN), (v_ref, v_buf, WIN), (q_ref, q_buf, 0))
    early = [
        pltpu.make_async_copy(gu_ref.at[0, 0], gu_buf, local_sem.at[0]),
        pltpu.make_async_copy(down_ref.at[0, 0], down_buf, local_sem.at[1]),
    ]
    local = [
        pltpu.make_async_copy(src.at[0, :, block(h)], dst.at[rows(h, base)], local_sem.at[2 + n])
        for n, (src, dst, base) in enumerate(streams)
    ]
    local += [
        pltpu.make_async_copy(src, dst, local_sem.at[5 + n])
        for n, (src, dst) in enumerate(
            (
                (fresh_gu_ref.at[0], fgu_buf),
                (fresh_down_ref.at[0], fdown_buf),
                (rates_ref.at[0], rate_ref),
                (gains_ref, gain_ref),
                (seqs_ref, seq_ref),
                (lens_ref, len_ref),
            )
        )
    ]
    for copy in early + local:
        copy.start()
    for copy in early:
        copy.wait()

    def encode(matrix, code, row):
        largest = jnp.maximum(jnp.max(jnp.abs(matrix), axis=0, keepdims=True), 1e-30)
        code[...] = jnp.round(matrix * (STEPS / largest)).astype(jnp.int32).astype(jnp.int16)
        scale_code[row : row + 1, : matrix.shape[1]] = largest * (1.0 / STEPS)

    def decode(code, row):
        return code.astype(jnp.int32).astype(jnp.float32) * scale_in[row : row + 1, : code.shape[1]]

    scale_code[...] = jnp.zeros_like(scale_code)
    encode(gu_buf[0], gu_code.at[0], 0)
    encode(gu_buf[1], gu_code.at[1], 1)
    encode(down_buf[...], down_code, 2)

    @pl.when(origin | middle)
    def _():
        pl.semaphore_wait(barrier, n_peer + 2)

    @pl.when(jnp.logical_not(origin | middle))
    def _():
        pl.semaphore_wait(barrier, n_peer + 1)


    receives = {}
    token_sends, ctx_sends = [], []

    def remote(name, group, src, dst, there, sem, here):
        def describe(at):
            return pltpu.make_async_remote_copy(
                src_ref=src, dst_ref=at, send_sem=send_sem.at[sem], recv_sem=recv_sem.at[sem],
                device_id=there, device_id_type=MESH,
            )

        group.append(describe(dst))
        receives.setdefault(name, []).append(describe(here))

    sem = 0
    for dz in (1, 0):
        for src, dst, base in streams:
            for n in range(n_peer):
                if PEERS[n][1] == dz:
                    out, back = to_peer[n], from_peer[n]
                    remote(
                        "tokens", token_sends, src.at[0, :, block(out)], dst.at[rows(h, base)],
                        (c, out), sem, dst.at[rows(back, base)],
                    )
                    sem += 1
    recent, older = pl.ds(WIN // 2, WIN // 2), pl.ds(0, WIN // 2)
    for name, src, dst in (
        ("state", scale_code, scale_in),
        ("state", gu_code, gu_in),
        ("state", down_code, down_in),
        ("recent", tail_k_ref.at[recent], k_buf.at[recent]),
        ("recent", tail_v_ref.at[recent], v_buf.at[recent]),
        ("older", tail_k_ref.at[older], k_buf.at[older]),
        ("older", tail_v_ref.at[older], v_buf.at[older]),
    ):
        remote(name, ctx_sends, src, dst, (succ, h), sem, dst)
        sem += 1
    sends = token_sends[3 * X_SIZE :] + ctx_sends
    tail_sends = ctx_sends[3:]
    detours, forwards = [], []
    for n, (src, dst) in enumerate(
        (
            (tail_k_ref.at[recent], k_buf.at[recent]),
            (tail_v_ref.at[recent], v_buf.at[recent]),
            (tail_k_ref.at[older], k_buf.at[older]),
            (tail_v_ref.at[older], v_buf.at[older]),
        )
    ):
        at = sem - 4 + n
        detours.append(
            pltpu.make_async_remote_copy(
                src_ref=src, dst_ref=relay_buf.at[n], send_sem=send_sem.at[at],
                recv_sem=relay_recv_sem.at[n], device_id=middle_id, device_id_type=MESH,
            )
        )
        forwards.append(
            pltpu.make_async_remote_copy(
                src_ref=relay_buf.at[n], dst_ref=dst, send_sem=relay_send_sem.at[n],
                recv_sem=recv_sem.at[at], device_id=final_id, device_id_type=MESH,
            )
        )

    far = lax.rem(c, 2) == 1
    z = (at_row // 2) * Z_SIZE + hz

    def chosen(stage):
        picked = c < 0 if stage else jnp.logical_not(far)
        for at, planned in enumerate(PLAN):
            if planned == stage:
                picked = picked | ((z == at) & far)
        return picked

    def start_ctx(stage):
        when = chosen(stage)

        @pl.when(when)
        def _():
            for copy in ctx_sends[:3]:
                copy.start()

        @pl.when(when & jnp.logical_not(origin))
        def _():
            for copy in tail_sends:
                copy.start()

    crossing = token_sends[: 3 * X_SIZE]
    waits = chosen(2)

    def drain(when):
        @pl.when(when)
        def _():
            for copy in crossing:
                copy.wait_send()

    @pl.when(origin)
    def _():
        for copy in detours:
            copy.start()

    start_ctx(0)
    for copy in token_sends:
        copy.start()
    start_ctx(1)
    drain(waits)
    start_ctx(2)

    @pl.when(middle)
    def _():
        for arriving, copy in zip(detours, forwards):
            arriving.wait_recv()
            copy.start()

    for copy in local:
        copy.wait()
    length = len_ref[0, c]
    linked = (seq_ref[1, c] == seq_ref[0, pred]).astype(jnp.int32)
    gain = gain_ref[...]
    exponent_scale = math.log2(math.e) / math.sqrt(HD)

    def attend(start):
        cols = WIN + TILE
        scores = nt(q_buf[pl.ds(start, TILE)], k_buf[pl.ds(start, cols)])
        key_pos = start - WIN + lax.broadcasted_iota(jnp.int32, (1, cols), 1)
        usable = jnp.where(key_pos < length, 1, 0) * jnp.where(key_pos >= 0, 1, linked)
        bias = jnp.where(usable > 0, 0.0, NEG)
        row = lax.broadcasted_iota(jnp.int32, (TILE, TILE), 0)
        col = lax.broadcasted_iota(jnp.int32, (TILE, TILE), 1)
        pieces = []
        for at in range(0, cols, TILE):
            own = scores[:, at : at + TILE]
            masked = own + bias[:, at : at + TILE]
            if at == 0:
                masked = jnp.where(col > row, masked, NEG)
            elif at == WIN:
                masked = jnp.where(col < row, masked, jnp.where(col == row, own, NEG))
            pieces.append(masked)
        scores = jnp.concatenate(pieces, axis=1)
        largest = jnp.max(scores, axis=-1, keepdims=True)
        exponent = jnp.exp2((scores - largest) * exponent_scale)
        total = jnp.sum(exponent, axis=-1, keepdims=True)
        weights = (exponent * (1.0 / total)).astype(jnp.bfloat16)
        return nn(weights, v_buf[pl.ds(start, cols)])

    for copy in receives["tokens"]:
        copy.wait_recv()
    start_ctx(3)
    for start in range(WIN, BLOCK, TILE):
        part_buf[pl.ds(start, TILE)] = attend(start)

    for copy in receives["state"]:
        copy.wait_recv()
    w_gate = jnp.where(linked > 0, decode(gu_in[0], 0), fgu_buf[0])
    w_up = jnp.where(linked > 0, decode(gu_in[1], 1), fgu_buf[1])
    w_down = jnp.where(linked > 0, decode(down_in[...], 2), fdown_buf[...])
    down_high, down_low = split(w_down)
    gate_high, gate_low = split(w_gate)
    up_high, up_low = split(w_up)
    in_weights = jnp.concatenate(
        [
            jnp.concatenate([gate_high, up_high], axis=1),
            jnp.concatenate([gate_low, up_low], axis=1),
        ],
        axis=0,
    )
    out_weights = jnp.concatenate([down_high, down_low], axis=1)

    def fast(start):
        own = q_buf[pl.ds(start, TILE)]
        wide = own.astype(jnp.float32)
        unit = lax.rsqrt(jnp.mean(wide * wide, axis=-1, keepdims=True) + EPS)
        hidden = nn(jnp.concatenate([own, own], axis=1), in_weights) * unit
        gate, up = hidden[:, :HID], hidden[:, HID:]
        act_high, act_low = split(gate * sigmoid(gate) * up)
        both = nn(act_high, out_weights)
        result = both[:, :HD] + both[:, HD:] + nn(act_low, down_high)
        scale = lax.rsqrt(jnp.mean(result * result, axis=-1, keepdims=True) + EPS)
        return result * scale * gain

    def finish(start, value):
        live = (start + lax.broadcasted_iota(jnp.int32, (TILE, 1), 0)) < length
        out_buf[pl.ds(start, TILE)] = jnp.where(live, value, 0.0).astype(jnp.bfloat16)

    out_receives = [
        pltpu.make_async_remote_copy(
            src_ref=out_buf.at[rows(out, 0)], dst_ref=mixed_ref.at[0, :, block(back)],
            send_sem=out_send_sem.at[n], recv_sem=out_recv_sem.at[n],
            device_id=(c, out), device_id_type=MESH,
        )
        for n, (out, back) in enumerate(zip(to_peer, from_peer))
    ]
    out_sends = [
        pltpu.make_async_remote_copy(
            src_ref=out_buf.at[rows(out, 0)], dst_ref=mixed_ref.at[0, :, block(h)],
            send_sem=out_send_sem.at[n], recv_sem=out_recv_sem.at[n],
            device_id=(c, out), device_id_type=MESH,
        )
        for n, out in enumerate(to_peer)
    ]
    own_part = pltpu.make_async_copy(
        out_buf.at[rows(h, 0)], mixed_ref.at[0, :, block(h)], local_sem.at[0]
    )

    def send_rows(start, stop):
        for copy, out in [*zip(out_sends, to_peer), (own_part, h)]:
            @pl.when((out >= start // HD) & (out < stop // HD))
            def _():
                copy.start()

    def first_rows_fast():
        for start in range(0, WIN, TILE):
            part_buf[pl.ds(start, TILE)] = fast(start)

    def first_rows(start):
        finish(start, part_buf[pl.ds(start, TILE)] + attend(start))
        send_rows(start, start + TILE)

    def last_rows():
        for start in range(WIN, BLOCK, TILE):
            finish(start, part_buf[pl.ds(start, TILE)] + fast(start))
        send_rows(WIN, BLOCK)

    @pl.when(hz == 0)
    def _():
        last_rows()
        first_rows_fast()
        for copy in receives["recent"]:
            copy.wait_recv()
        first_rows(TILE)
        for copy in receives["older"]:
            copy.wait_recv()
        first_rows(0)

    @pl.when(hz != 0)
    def _():
        first_rows_fast()
        for copy in receives["recent"] + receives["older"]:
            copy.wait_recv()
        first_rows(0)
        first_rows(TILE)
        last_rows()

    key_weights = jnp.concatenate(
        [
            jnp.concatenate(split(w_gate.T), axis=1),
            jnp.concatenate(split(w_up.T), axis=1),
        ],
        axis=0,
    )
    ones = jnp.ones((8, 2 * HD), jnp.bfloat16)
    grad_in = jnp.zeros((2 * HID, HD), jnp.float32)
    grad_down = jnp.zeros((HID, HD), jnp.float32)
    for start in range(0, BLOCK, TILE):
        key = k_buf[pl.ds(WIN + start, TILE)]
        value = v_buf[pl.ds(WIN + start, TILE)]
        wide = key.astype(jnp.float32)
        squares = nt(ones, jnp.concatenate(split(wide * wide), axis=1))[0:1]
        unit = lax.rsqrt(squares * (1.0 / HD) + EPS)
        token = start + lax.broadcasted_iota(jnp.int32, (1, TILE), 1)
        rate = jnp.where(token < length, rate_ref[:, pl.ds(start, TILE)], 0.0)
        hidden = nt(key_weights, jnp.concatenate([key, key], axis=1)) * unit
        gate, up = hidden[:HID], hidden[HID:]
        s = sigmoid(gate)
        act = gate * s
        back = nt(out_weights, jnp.concatenate([value, value], axis=1)) * rate
        grad_down += nn((act * up * rate).astype(jnp.bfloat16), value)
        back = back * unit
        factor = jnp.concatenate([back * up * s * (1.0 + gate * (1.0 - s)), back * act], axis=0)
        grad_in += nn(factor.astype(jnp.bfloat16), key)

    def renormed(old, new):
        old_mean = jnp.mean(old * old, axis=0, keepdims=True) + EPS
        new_mean = jnp.mean(new * new, axis=0, keepdims=True) + EPS
        return new * (jnp.sqrt(old_mean) * lax.rsqrt(new_mean))

    gu_out_ref[0, 0, 0] = renormed(w_gate, w_gate + grad_in[:HID].T)
    gu_out_ref[0, 0, 1] = renormed(w_up, w_up + grad_in[HID:].T)
    down_out_ref[0, 0] = renormed(w_down, w_down + grad_down)

    own_part.wait()
    drain(jnp.logical_not(waits))

    @pl.when(middle)
    def _():
        for copy in forwards:
            copy.wait_send()

    for copy in sends + out_sends:
        copy.wait_send()
    for copy in out_receives:
        copy.wait_recv()


def solution(mesh):
    ctx_count = mesh.shape["ctx"]
    n_remote = 3 * len(PEERS) + 7

    def on_device(
        queries, keys, values, rates, tail_keys, tail_values, state_in_gu, state_in_down,
        fresh_gu, fresh_down, out_gain, seq_ids, live_lengths,
    ):
        hbm = pl.BlockSpec(memory_space=pltpu.HBM)
        vmem = pl.BlockSpec(memory_space=pltpu.VMEM)

        def body(*refs):
            kernel(ctx_count, *refs)

        results = pl.pallas_call(
            body,
            name="layer",
            out_shape=(
                jax.ShapeDtypeStruct(queries.shape, jnp.bfloat16),
                jax.ShapeDtypeStruct(state_in_gu.shape, jnp.float32),
                jax.ShapeDtypeStruct(state_in_down.shape, jnp.float32),
            ),
            in_specs=[hbm] * 13,
            out_specs=(vmem, vmem, vmem),
            scratch_shapes=[
                pltpu.VMEM((BLOCK, HD), jnp.bfloat16),
                pltpu.VMEM((WIN + BLOCK, HD), jnp.bfloat16),
                pltpu.VMEM((WIN + BLOCK, HD), jnp.bfloat16),
                pltpu.VMEM((2, HD, HID), jnp.float32),
                pltpu.VMEM((HID, HD), jnp.float32),
                pltpu.VMEM((2, HD, HID), jnp.float32),
                pltpu.VMEM((HID, HD), jnp.float32),
                pltpu.VMEM((BLOCK, HD), jnp.bfloat16),
                pltpu.VMEM((BLOCK, HD), jnp.float32),
                pltpu.VMEM((2, HD, HID), jnp.int16),
                pltpu.VMEM((HID, HD), jnp.int16),
                pltpu.VMEM((8, HID), jnp.float32),
                pltpu.VMEM((2, HD, HID), jnp.int16),
                pltpu.VMEM((HID, HD), jnp.int16),
                pltpu.VMEM((8, HID), jnp.float32),
                pltpu.VMEM((1, BLOCK), jnp.float32),
                pltpu.VMEM((1, HD), jnp.float32),
                pltpu.SMEM((2, ctx_count), jnp.int32),
                pltpu.SMEM((1, ctx_count), jnp.int32),
                pltpu.VMEM((4, WIN // 2, HD), jnp.bfloat16),
                pltpu.SemaphoreType.DMA((11,)),
                pltpu.SemaphoreType.DMA((n_remote,)),
                pltpu.SemaphoreType.DMA((n_remote,)),
                pltpu.SemaphoreType.DMA((len(PEERS),)),
                pltpu.SemaphoreType.DMA((len(PEERS),)),
                pltpu.SemaphoreType.DMA((4,)),
                pltpu.SemaphoreType.DMA((4,)),
            ],
            compiler_params=pltpu.CompilerParams(
                collective_id=0, has_side_effects=True, vmem_limit_bytes=40 * 1024 * 1024
            ),
        )(
            *[
                pltpu.with_memory_space_constraint(array, pltpu.HBM)
                for array in (
                    queries, keys, values, rates, tail_keys, tail_values, state_in_gu, state_in_down,
                    fresh_gu, fresh_down, out_gain[None], seq_ids.T, live_lengths.T,
                )
            ]
        )

        def store(*refs):
            mixed, pair, down, mixed_out, pair_out, down_out, sem = refs
            parts = [
                (mixed.at[0, pl.ds(at, 32)], mixed_out.at[0, pl.ds(at, 32)]) for at in range(0, HD, 32)
            ]
            for at in range(0, HD, HD // 2):
                for n in range(2):
                    cut = pl.ds(at, HD // 2)
                    parts.append((pair.at[0, 0, n, cut], pair_out.at[0, 0, n, cut]))
            for at in range(0, HID, HD):
                parts.append((down.at[0, 0, pl.ds(at, HD)], down_out.at[0, 0, pl.ds(at, HD)]))
            copies = [pltpu.make_async_copy(a, b, sem.at[n]) for n, (a, b) in enumerate(parts)]
            for copy in copies:
                copy.start()
            for copy in copies:
                copy.wait()

        return pl.pallas_call(
            store,
            name="store",
            out_shape=tuple(jax.ShapeDtypeStruct(r.shape, r.dtype) for r in results),
            in_specs=[vmem] * 3,
            out_specs=[hbm] * 3,
            scratch_shapes=[pltpu.SemaphoreType.DMA((10,))],
            compiler_params=pltpu.CompilerParams(vmem_limit_bytes=8 * 1024 * 1024),
        )(*results)

    placed = (
        P(None, ("ctx", "head"), None),
        P(None, ("ctx", "head"), None),
        P(None, ("ctx", "head"), None),
        P(None, "head", "ctx"),
        P("ctx", "head"),
        P("ctx", "head"),
        P("ctx", "head", None, None, None),
        P("ctx", "head", None, None),
        P("head", None, None, None),
        P("head", None, None),
        P("head"),
        P(),
        P(),
    )
    return jax.shard_map(
        on_device,
        mesh=mesh,
        in_specs=placed,
        out_specs=(
            P(None, ("ctx", "head"), None),
            P("ctx", "head", None, None, None),
            P("ctx", "head", None, None),
        ),
        check_vma=False,
    )
```
